128 devices in a mesh: row: 8 (over z, x_lo), col: 16 (over x_hi, y, core).
Axes of the slice: x: 4 (x_hi: 2, x_lo: 2; x = x_hi * 2 + x_lo), y: 4, z: 4, core: 2. Of those that a mesh axis runs over, the one named last changes fastest.
Arguments:
- stream: float32 [16384, 256], P(('row', 'col')), may hold values from -130 to 130
- stream_tail: float32 [31, 256], replicated, may hold values from -130 to 130
- archive: float32 [65536, 256], P(('col', 'row')), may hold values from -60 to 60
- archive_tail: float32 [31, 256], replicated, may hold values from -60 to 60
Outputs:
- row_profile: float32 [16384], P(('row', 'col'))
- col_profile: float32 [65536], P(('col', 'row'))
The draws below stay inside these ranges and needn't reach their ends.
All inputs are finite; a program needn't handle non-finite values.
Results may differ from the reference program's by a relative error of at most 0.0003.
Values sent between devices are 32-bit elements; how exact they have to be, the bound alone decides.
A program may use at most 128 MiB of HBM per device.

```python
import jax
import jax.numpy as jnp
from jax import lax

D = 256
M = 32
SEG = 64
NA = 16384
NB = 65536


def make_frames(key):
    keys = jax.random.split(jax.random.fold_in(key, 7), 8)
    stream_len = NA + M - 1
    archive_len = NB + M - 1
    archive_raw = jnp.clip(jax.random.normal(keys[0], (archive_len, D), jnp.float32), -5.0, 5.0)
    runs = (stream_len + SEG - 1) // SEG
    offsets = jax.random.randint(keys[1], (runs,), 0, archive_len - SEG + 1)
    source = (offsets[:, None] + jnp.arange(SEG)[None, :]).reshape(-1)[:stream_len]
    noise = jnp.clip(jax.random.normal(keys[2], (stream_len, D), jnp.float32), -5.0, 5.0)
    fresh = jnp.clip(jax.random.normal(keys[6], (stream_len, D), jnp.float32), -5.0, 5.0)
    matched = jax.random.randint(keys[7], (runs,), 0, 2)
    matched = jnp.repeat(matched, SEG, total_repeat_length=runs * SEG)[:stream_len][:, None]
    copied = archive_raw[source] + noise
    stream_raw = jnp.where(matched == 1, copied, fresh)
    return (stream_raw, archive_raw)


def draw_stream(key, part):
    return make_frames(key)[0][:NA]


def draw_stream_tail(key, part):
    return make_frames(key)[0][NA:]


def draw_archive(key, part):
    return make_frames(key)[1][:NB]


def draw_archive_tail(key, part):
    return make_frames(key)[1][NB:]


def setup_inputs(seed: int = 0) -> dict:
    arg_keys = jax.random.split(jax.random.key(seed), 5)
    stream = draw_stream(jax.random.fold_in(arg_keys[4], 71), 0)
    stream_tail = draw_stream_tail(jax.random.fold_in(arg_keys[4], 71), 0)
    archive = draw_archive(jax.random.fold_in(arg_keys[4], 71), 0)
    archive_tail = draw_archive_tail(jax.random.fold_in(arg_keys[4], 71), 0)
    return {"stream": stream, "stream_tail": stream_tail, "archive": archive, "archive_tail": archive_tail}


def to_unit(frames):
    return frames / jnp.sqrt(lax.optimization_barrier(jnp.sum(frames * frames, axis=1, keepdims=True)) + 1e-06)

def window_sum(gram_block):
    summed = gram_block
    width = 1
    while width < M:
        height = summed.shape[0] - width
        breadth = summed.shape[1] - width
        summed = summed[0:height, 0:breadth] + summed[width:, width:]
        width = width * 2
    return summed

def profile_tile(stream_ext, archive_ext):
    row_count = stream_ext.shape[0] - (M - 1)
    col_count = archive_ext.shape[0] - (M - 1)
    block_rows = min(256, row_count)
    while block_rows * col_count < 2 ** 20 and row_count % (block_rows * 2) == 0:
        block_rows = block_rows * 2
    steps_count = row_count // block_rows

    def advance(col_best, position):
        first_row = (position * block_rows).astype(jnp.int32)
        window_rows = lax.dynamic_slice_in_dim(stream_ext, first_row, block_rows + M - 1, 0)
        gram_block = lax.dot_general(window_rows, archive_ext, (((1,), (1,)), ((), ())), precision=lax.Precision.HIGHEST, preferred_element_type=jnp.float32)
        scores = window_sum(gram_block) / M
        return (jnp.maximum(col_best, lax.optimization_barrier(jnp.max(scores, axis=0))), lax.optimization_barrier(jnp.max(scores, axis=1)))
    start_best = jnp.full((col_count,), -2.0, jnp.float32)
    col_best, row_best = lax.scan(advance, start_best, jnp.arange(steps_count, dtype=jnp.int32))
    return (row_best.reshape(-1), col_best)

def reference(stream, stream_tail, archive, archive_tail):
    stream_ext = to_unit(jnp.concatenate([stream, stream_tail], axis=0))
    archive_ext = to_unit(jnp.concatenate([archive, archive_tail], axis=0))
    row_profile, col_profile = profile_tile(stream_ext, archive_ext)
    return (row_profile, col_profile)
```

```python
import functools

import jax
import jax.numpy as jnp
from jax import lax
from jax.sharding import PartitionSpec as P
from jax.experimental import pallas as pl
from jax.experimental.pallas import tpu as pltpu
M=32; C=17; SEG=512; T=544; TV=512; PAD=32
NEG=-2.0*32
def prep_rhs(u_ref, b_ref):
    def one(c,_):
        xt = jnp.concatenate([u_ref.at[h][pl.ds(c, 128, stride=C), :].T for h in range(2)], axis=0)
        hi = xt.astype(jnp.bfloat16)
        lo = (xt - hi.astype(jnp.float32)).astype(jnp.bfloat16)
        n = pl.multiple_of(c*128,128)
        b_ref[0:256, pl.ds(n,128)] = hi
        b_ref[256:512, pl.ds(n,128)] = lo
        b_ref[512:768, pl.ds(n,128)] = hi
        return 0
    lax.fori_loop(0, C, one, 0)
def prep_lhs(v_ref, a_ref, t0, nt):
    def one(i,_):
        t = t0 + i*2
        x = jnp.concatenate([jnp.concatenate([v_ref.at[h][pl.ds(t+k, 8, stride=SEG), :] for k in range(2)], axis=0) for h in range(2)], axis=1)
        hi = x.astype(jnp.bfloat16)
        lo = (x - hi.astype(jnp.float32)).astype(jnp.bfloat16)
        r = pl.multiple_of(t*8, 16)
        a_ref[pl.ds(r,16), 0:256] = hi
        a_ref[pl.ds(r,16), 256:512] = hi
        a_ref[pl.ds(r,16), 512:768] = lo
        return 0
    lax.fori_loop(0, nt//2, one, 0, unroll=4)
DN = (((1,), (0,)), ((), ()))
def mm(a_ref, b_ref, g_ref, t0, nt, n, nw):
    r = pl.multiple_of(t0*8, 16)
    ro = pl.multiple_of((t0+PAD)*8, 16)
    g_ref[pl.ds(ro, nt*8), pl.ds(n, nw)] = lax.dot_general(a_ref[pl.ds(r, nt*8), :], b_ref[:, pl.ds(n, nw)], DN, preferred_element_type=jnp.float32)
def vstep(g_ref, t, E, R, tm_ref, out):
    row = pl.multiple_of((t+PAD)*8, 8)
    old = pl.multiple_of(t*8, 8)
    N = []
    for c in range(C):
        g = g_ref[pl.ds(row,8), c*128:(c+1)*128]
        tile, sh = (c+2, 2) if c+2 < C else (c+2-C, 1)
        go = pltpu.roll(g_ref[pl.ds(old,8), tile*128:(tile+1)*128], sh, 1)
        ep = E[c-1] if c else pltpu.roll(E[C-1], 1, 1)
        N.append(ep + (g - go))
    if out:
        R = [jnp.maximum(r, e) for r, e in zip(R, N)]
        mx = functools.reduce(jnp.maximum, N[5:14])
        mb = functools.reduce(jnp.maximum, N[0:5])
        mc = functools.reduce(jnp.maximum, N[14:17])
        lane = lax.broadcasted_iota(jnp.int32, (8,128), 1)
        neg = jnp.float32(NEG)
        mid = (lane >= 2) & (lane <= 121)
        m = jnp.where(mid, mx, neg)
        m = jnp.maximum(m, jnp.where((lane>=2)&(lane<=122), mb, neg))
        m = jnp.maximum(m, jnp.where((lane>=1)&(lane<=121), mc, neg))
        tm_ref[pl.ds(pl.multiple_of((t-31)*8,8), 8), :] = m
    return N, R
def compute(a_ref, b_ref, g_ref, tm_ref, NT=2):
    zero = jnp.zeros((8,128), jnp.float32)
    g_ref[0:PAD*8, :] = jnp.zeros((PAD*8, C*128), jnp.float32)
    lax.fori_loop(0, 8, lambda j,_: (mm(a_ref,b_ref,g_ref,0,96,pl.multiple_of(j*256,256),256),0)[1], 0)
    mm(a_ref,b_ref,g_ref,0,96,2048,128)
    E=[zero]*C; R=[jnp.full((8,128),NEG,jnp.float32)]*C
    def warm(t, c):
        n,_ = vstep(g_ref, t, list(c), R, tm_ref, False)
        return tuple(n)
    E = lax.fori_loop(0, 31, warm, tuple(E))
    def blk(b, carry):
        t0 = 96+64*b
        def inner(j, carry):
            E,R = list(carry[0]), list(carry[1])
            mm(a_ref,b_ref,g_ref,t0,64,pl.multiple_of(j*256*NT,256),256*NT)
            for k in range(8*NT):
                E,R = vstep(g_ref, 31+64*b + j*8*NT + k, E, R, tm_ref, True)
            return tuple(E), tuple(R)
        carry = lax.fori_loop(0, 8//NT, inner, carry)
        mm(a_ref,b_ref,g_ref,t0,64,2048,128)
        return carry
    carry = lax.fori_loop(0, 7, blk, (tuple(E),tuple(R)))
    def fin(j, carry):
        E,R = list(carry[0]), list(carry[1])
        for k in range(8):
            E,R = vstep(g_ref, 31+448 + j*8 + k, E, R, tm_ref, True)
        return tuple(E), tuple(R)
    E,R = lax.fori_loop(0, 8, fin, carry)
    return R
def finish(tm_ref, R, col_ref, row_ref):
    def one(s,_):
        rows=[]
        for tb in range(4):
            x = tm_ref[pl.ds(s + tb*1024, 128, stride=8), :]
            rows.append(jnp.max(x.T, axis=0, keepdims=True))
        col_ref[pl.ds(s,1),:] = jnp.concatenate(rows, axis=1)*(1.0/M)
        return 0
    lax.fori_loop(0, 8, one, 0)
    for c in range(C):
        row_ref[c:c+1,:] = jnp.max(R[c], axis=0, keepdims=True)*(1.0/M)
    row_ref[C:24,:] = jnp.full((7,128), -2.0, jnp.float32)

def kern(v_ref, u_ref, col_ref, row_ref, a, b, g, tm):
    prep_rhs(u_ref, b)
    prep_lhs(v_ref, a, 0, T)
    R = compute(a, b, g, tm, 4)
    finish(tm, R, col_ref, row_ref)

def call(v, u):
    vm = pl.BlockSpec(memory_space=pltpu.VMEM)
    return pl.pallas_call(
        kern,
        out_shape=(jax.ShapeDtypeStruct((8, 512), jnp.float32), jax.ShapeDtypeStruct((24, 128), jnp.float32)),
        in_specs=[vm, vm], out_specs=(vm, vm),
        scratch_shapes=[
            pltpu.VMEM((T*8, 768), jnp.bfloat16),
            pltpu.VMEM((768, C*128), jnp.bfloat16),
            pltpu.VMEM(((T+PAD)*8, C*128), jnp.float32),
            pltpu.VMEM((TV*8, 128), jnp.float32),
        ],
        compiler_params=pltpu.CompilerParams(vmem_limit_bytes=67043328),
        name="profile_tile")(v, u)

def to_unit(frames):
    return frames / jnp.sqrt(jnp.sum(frames * frames, axis=1, keepdims=True) + 1e-06)

def planes(x, rows):
    x = jnp.pad(x, ((0, rows - x.shape[0]), (0, 0)))
    return jnp.stack([x[:, :128], x[:, 128:]])

def on_device(stream, stream_tail, archive, archive_tail):
    r, c = lax.axis_index("row"), lax.axis_index("col")
    nr, nc = lax.axis_size("row"), lax.axis_size("col")
    su, au = to_unit(stream), to_unit(archive)
    st, at = to_unit(stream_tail), to_unit(archive_tail)
    s_blk = lax.all_gather(su, "col", axis=0, tiled=True)
    a_blk = lax.all_gather(au, "row", axis=0, tiled=True)
    s_head = lax.ppermute(s_blk[:31], "row", [(i, i - 1) for i in range(1, nr)])
    a_head = lax.ppermute(a_blk[:31], "col", [(i, i - 1) for i in range(1, nc)])
    s_head = jnp.where(r == nr - 1, st, s_head)
    a_head = jnp.where(c == nc - 1, at, a_head)
    u = planes(jnp.concatenate([s_blk, s_head]), C*128)
    v = planes(jnp.concatenate([a_blk, a_head]), 4128)
    col, row = call(v, u)
    row = row[:C].T.reshape(-1)[31:31 + 2048].reshape(16, 128)
    row = jnp.max(lax.all_to_all(row, "col", 0, 0, tiled=True), axis=0)
    col = jnp.max(lax.all_to_all(col, "row", 0, 0, tiled=True), axis=0)
    return row, col

def solution(mesh):
    return jax.shard_map(
        on_device, mesh=mesh,
        in_specs=(P(("row", "col"), None), P(), P(("col", "row"), None), P()),
        out_specs=(P(("row", "col")), P(("col", "row"))),
        check_vma=False)
```

```python
import functools

import jax
import jax.numpy as jnp
from jax import lax
from jax.sharding import PartitionSpec as P
from jax.experimental import pallas as pl
from jax.experimental.pallas import tpu as pltpu
M=32; C=17; SEG=512; T=544; TV=512; PAD=32
NEG=-2.0*32
def prep_rhs(u_ref, b_ref):
    def one(c,_):
        xt = jnp.concatenate([u_ref.at[h][pl.ds(c, 128, stride=C), :].T for h in range(2)], axis=0)
        hi = xt.astype(jnp.bfloat16)
        lo = (xt - hi.astype(jnp.float32)).astype(jnp.bfloat16)
        n = pl.multiple_of(c*128,128)
        b_ref[0:256, pl.ds(n,128)] = hi
        b_ref[256:512, pl.ds(n,128)] = lo
        b_ref[512:768, pl.ds(n,128)] = hi
        return 0
    lax.fori_loop(0, C, one, 0)
def prep_lhs(v_ref, a_ref, t0, nt):
    def one(i,_):
        t = t0 + i*2
        x = jnp.concatenate([jnp.concatenate([v_ref.at[h][pl.ds(t+k, 8, stride=SEG), :] for k in range(2)], axis=0) for h in range(2)], axis=1)
        hi = x.astype(jnp.bfloat16)
        lo = (x - hi.astype(jnp.float32)).astype(jnp.bfloat16)
        r = pl.multiple_of(t*8, 16)
        a_ref[pl.ds(r,16), 0:256] = hi
        a_ref[pl.ds(r,16), 256:512] = hi
        a_ref[pl.ds(r,16), 512:768] = lo
        return 0
    lax.fori_loop(0, nt//2, one, 0, unroll=4)
DN = (((1,), (0,)), ((), ()))
def mm(a_ref, b_ref, g_ref, t0, nt, n, nw):
    r = pl.multiple_of(t0*8, 16)
    ro = pl.multiple_of((t0+PAD)*8, 16)
    g_ref[pl.ds(ro, nt*8), pl.ds(n, nw)] = lax.dot_general(a_ref[pl.ds(r, nt*8), :], b_ref[:, pl.ds(n, nw)], DN, preferred_element_type=jnp.float32)
def vstep(g_ref, t, E, R, tm_ref, out):
    row = pl.multiple_of((t+PAD)*8, 8)
    old = pl.multiple_of(t*8, 8)
    N = []
    for c in range(C):
        g = g_ref[pl.ds(row,8), c*128:(c+1)*128]
        tile, sh = (c+2, 2) if c+2 < C else (c+2-C, 1)
        go = pltpu.roll(g_ref[pl.ds(old,8), tile*128:(tile+1)*128], sh, 1)
        ep = E[c-1] if c else pltpu.roll(E[C-1], 1, 1)
        N.append(ep + (g - go))
    if out:
        R = [jnp.maximum(r, e) for r, e in zip(R, N)]
        mx = functools.reduce(jnp.maximum, N[5:14])
        mb = functools.reduce(jnp.maximum, N[0:5])
        mc = functools.reduce(jnp.maximum, N[14:17])
        lane = lax.broadcasted_iota(jnp.int32, (8,128), 1)
        neg = jnp.float32(NEG)
        mid = (lane >= 2) & (lane <= 121)
        m = jnp.where(mid, mx, neg)
        m = jnp.maximum(m, jnp.where((lane>=2)&(lane<=122), mb, neg))
        m = jnp.maximum(m, jnp.where((lane>=1)&(lane<=121), mc, neg))
        tm_ref[pl.ds(pl.multiple_of((t-31)*8,8), 8), :] = m
    return N, R
def compute(a_ref, b_ref, g_ref, tm_ref, NT=2):
    zero = jnp.zeros((8,128), jnp.float32)
    g_ref[0:PAD*8, :] = jnp.zeros((PAD*8, C*128), jnp.float32)
    lax.fori_loop(0, 8, lambda j,_: (mm(a_ref,b_ref,g_ref,0,96,pl.multiple_of(j*256,256),256),0)[1], 0)
    mm(a_ref,b_ref,g_ref,0,96,2048,128)
    E=[zero]*C; R=[jnp.full((8,128),NEG,jnp.float32)]*C
    def warm(t, c):
        n,_ = vstep(g_ref, t, list(c), R, tm_ref, False)
        return tuple(n)
    E = lax.fori_loop(0, 31, warm, tuple(E))
    def blk(b, carry):
        t0 = 96+64*b
        def inner(j, carry):
            E,R = list(carry[0]), list(carry[1])
            mm(a_ref,b_ref,g_ref,t0,64,pl.multiple_of(j*256*NT,256),256*NT)
            for k in range(8*NT):
                E,R = vstep(g_ref, 31+64*b + j*8*NT + k, E, R, tm_ref, True)
            return tuple(E), tuple(R)
        carry = lax.fori_loop(0, 8//NT, inner, carry)
        mm(a_ref,b_ref,g_ref,t0,64,2048,128)
        return carry
    carry = lax.fori_loop(0, 7, blk, (tuple(E),tuple(R)))
    def fin(j, carry):
        E,R = list(carry[0]), list(carry[1])
        for k in range(8):
            E,R = vstep(g_ref, 31+448 + j*8 + k, E, R, tm_ref, True)
        return tuple(E), tuple(R)
    E,R = lax.fori_loop(0, 8, fin, carry)
    return R
def finish(tm_ref, R, col_ref, row_ref):
    def one(s, _):
        for tb in range(4):
            x = tm_ref[pl.ds(s + tb*1024, 128, stride=8), :]
            col_ref[s, 0:1, tb*128:(tb+1)*128] = jnp.max(x.T, axis=0, keepdims=True)*(1.0/M)
        return 0
    lax.fori_loop(0, 8, one, 0)
    rows = jnp.concatenate([jnp.max(r, axis=0, keepdims=True) for r in R] + [jnp.full((7, 128), NEG, jnp.float32)], axis=0)*(1.0/M)
    for j in range(4):
        q = lax.broadcasted_iota(jnp.int32, (128, 512), 1) + (31 + 512*j)
        pick = (lax.broadcasted_iota(jnp.int32, (128, 512), 0) == ((q*3856) >> 16)).astype(jnp.float32)
        x = lax.dot_general(rows, pick, DN, precision=lax.Precision.HIGHEST, preferred_element_type=jnp.float32)
        q = lax.broadcasted_iota(jnp.int32, (24, 512), 1) + (31 + 512*j)
        lane = (q*3856) >> 16
        x = jnp.where(lax.broadcasted_iota(jnp.int32, (24, 512), 0) == q - lane*C, x, 0.0)
        x = jnp.sum(x, axis=0, keepdims=True)
        for m in range(4):
            row_ref[4*j + m, 0:1, :] = x[:, 128*m:128*(m+1)]

def kern(v_ref, u_ref, col_ref, row_ref, a, b, g, tm):
    prep_rhs(u_ref, b)
    prep_lhs(v_ref, a, 0, T)
    R = compute(a, b, g, tm, 4)
    finish(tm, R, col_ref, row_ref)

VM = pl.BlockSpec(memory_space=pltpu.VMEM)
ANY = pl.BlockSpec(memory_space=pl.ANY)
F32 = jnp.float32

def call(v, u):
    return pl.pallas_call(
        kern,
        out_shape=(jax.ShapeDtypeStruct((8, 1, 512), F32), jax.ShapeDtypeStruct((16, 1, 128), F32)),
        in_specs=[VM, VM], out_specs=(VM, VM),
        scratch_shapes=[
            pltpu.VMEM((T*8, 768), jnp.bfloat16),
            pltpu.VMEM((768, C*128), jnp.bfloat16),
            pltpu.VMEM(((T+PAD)*8, C*128), jnp.float32),
            pltpu.VMEM((TV*8, 128), jnp.float32),
        ],
        compiler_params=pltpu.CompilerParams(vmem_limit_bytes=67043328),
        name="profile_tile")(v, u)

MESH = pl.DeviceIdType.MESH

def place():
    row, col = lax.axis_index("row"), lax.axis_index("col")
    z, x_lo = row // 2, row % 2
    x_hi, y, k = col // 8, (col // 2) % 4, col % 2
    return row, col, x_hi, x_lo, y, z, k

def dev(x, y, z, k):
    return (z*2 + x % 2, (x // 2)*8 + y*2 + k)

def unit(x):
    return x / jnp.sqrt(jnp.sum(x*x, axis=1, keepdims=True) + 1e-06)

def put_planes(dst, x):
    dst[0] = x[:, :128]
    dst[1] = x[:, 128:]

NQ = 4
CH = 512 // NQ

def gather_kern(s_ref, st_ref, a_ref, at_ref, v_ref, u_ref, su, av, tails, zeros, send, got_v, got_u, misc):
    row, col, x_hi, x_lo, y, z, k = place()
    x = x_hi*2 + x_lo
    waits = []
    count = [0]

    def remote(src, dst, sem, to, when=None):
        c = pltpu.make_async_remote_copy(src_ref=src, dst_ref=dst, send_sem=send.at[count[0]], recv_sem=sem, device_id=to, device_id_type=MESH)
        count[0] += 1
        waits.append((c, when))
        if when is None:
            c.start()
        else:
            pl.when(when)(c.start)

    def arrived(ref, sem):
        pltpu.make_async_copy(ref, ref, sem).wait()

    def vs(b, q):
        return v_ref.at[:, pl.ds(pl.multiple_of(b*512 + q*CH, CH), CH), :]

    def us(b):
        return u_ref.at[:, pl.ds(pl.multiple_of(b*128, 128), 128), :]

    put_planes(av, unit(a_ref[...]))
    put_planes(su, unit(s_ref[...]))
    zero = jnp.zeros((1, 256), F32)
    put_planes(tails.at[0], jnp.concatenate([unit(st_ref[...]), zero], axis=0))
    put_planes(tails.at[1], jnp.concatenate([unit(at_ref[...]), zero], axis=0))
    zeros[...] = jnp.zeros(zeros.shape, F32)
    home = x_lo == k
    away = x_lo != k
    for q in range(NQ):
        src = av.at[:, pl.ds(q*CH, CH), :]
        local = pltpu.make_async_copy(src, vs(row, q), got_v.at[row, q])
        pl.when(home)(local.start)
        remote(src, vs(row, q), got_v.at[row, q], dev(x_hi*2 + k, y, z, 1 - k), away)
    own = pltpu.make_async_copy(su, us(col), got_u.at[col])
    pl.when(home)(own.start)
    remote(su, us(col), got_u.at[col], dev(x, y, z, 1 - k), away)
    for p in (1, 3, 2):
        remote(su, us(col), got_u.at[col], dev((x + p*k) % 4, (y + p*(1 - k)) % 4, z, x_lo))
    pad = pltpu.make_async_copy(zeros, u_ref.at[:, pl.ds(2080, 96), :], misc.at[0])
    pad.start()
    bo = z*2 + k
    up, dn, far = (z + 1) % 4, (z + 3) % 4, (z + 2) % 4
    for q in range(NQ):
        arrived(vs(bo, q), got_v.at[bo, q])
        remote(vs(bo, q), vs(bo, q), got_v.at[bo, q], dev(x, y, up, k))
        remote(vs(bo, q), vs(bo, q), got_v.at[bo, q], dev(x, y, dn, k))
        remote(vs(bo, q), vs(bo, q), got_v.at[bo, q], dev(x, y, z, 1 - k))
    for xs in range(2):
        b = xs*8 + y*2 + 1
        arrived(us(b), got_u.at[b])
        for p in (1, 3, 2):
            remote(us(b), us(b), got_u.at[b], dev(x, (y + p) % 4, z, k))
    for yy in range(4):
        b = x_hi*8 + yy*2
        pl.when(home)(lambda b=b: arrived(us(b), got_u.at[b]))
        for p in (1, 3, 2):
            remote(us(b), us(b), got_u.at[b], dev((x + p) % 4, y, z, k), home)
    bu, bd, bf = up*2 + k, dn*2 + k, far*2 + k
    for q in range(NQ):
        arrived(vs(bd, q), got_v.at[bd, q])
        if q % 2 == 0:
            remote(vs(bd, q), vs(bd, q), got_v.at[bd, q], dev(x, y, up, k))
        remote(vs(bd, q), vs(bd, q), got_v.at[bd, q], dev(x, y, z, 1 - k))
        arrived(vs(bu, q), got_v.at[bu, q])
        if q % 2 == 1:
            remote(vs(bu, q), vs(bu, q), got_v.at[bu, q], dev(x, y, dn, k))
        remote(vs(bu, q), vs(bu, q), got_v.at[bu, q], dev(x, y, z, 1 - k))
    for q in range(NQ):
        arrived(vs(bf, q), got_v.at[bf, q])
        remote(vs(bf, q), vs(bf, q), got_v.at[bf, q], dev(x, y, z, 1 - k))
    for zz in range(4):
        for q in range(NQ):
            b = zz*2 + 1 - k
            arrived(vs(b, q), got_v.at[b, q])
    for xs in range(2):
        for yy in range(4):
            b = xs*8 + yy*2 + 1
            pl.when(yy != y)(lambda b=b: arrived(us(b), got_u.at[b]))
            b = xs*8 + yy*2
            pl.when(jnp.logical_or(away, xs != x_hi))(lambda b=b: arrived(us(b), got_u.at[b]))
    cb = (x_hi*4 + y)*2 + x_lo
    pc = (cb + 15) % 16
    rb = z*2 + k
    pr = (rb + 7) % 8
    remote(v_ref.at[:, pl.ds(0, 32), :], v_ref.at[:, pl.ds(4096, 32), :], misc.at[1], dev((pc // 8)*2 + pc % 2, (pc // 2) % 4, z, k), cb != 0)
    remote(u_ref.at[:, pl.ds(0, 32), :], u_ref.at[:, pl.ds(2048, 32), :], misc.at[2], dev(x, y, pr // 2, pr % 2), rb != 0)
    tv = pltpu.make_async_copy(tails.at[1], v_ref.at[:, pl.ds(4096, 32), :], misc.at[1])
    tu = pltpu.make_async_copy(tails.at[0], u_ref.at[:, pl.ds(2048, 32), :], misc.at[2])
    pl.when(cb == 15)(tv.start)
    pl.when(rb == 7)(tu.start)
    tv.wait()
    tu.wait()
    pad.wait()
    for c, when in waits:
        if when is None:
            c.wait_send()
        else:
            pl.when(when)(c.wait_send)

def gather(s, st, a, at):
    return pl.pallas_call(
        gather_kern,
        out_shape=(jax.ShapeDtypeStruct((2, 4128, 128), F32), jax.ShapeDtypeStruct((2, 2176, 128), F32)),
        in_specs=[VM]*4, out_specs=(ANY, ANY),
        scratch_shapes=[
            pltpu.VMEM((2, 128, 128), F32), pltpu.VMEM((2, 512, 128), F32),
            pltpu.VMEM((2, 2, 32, 128), F32), pltpu.VMEM((2, 96, 128), F32),
            pltpu.SemaphoreType.DMA((72,)), pltpu.SemaphoreType.DMA((8, NQ)), pltpu.SemaphoreType.DMA((16,)), pltpu.SemaphoreType.DMA((3,)),
        ],
        compiler_params=pltpu.CompilerParams(has_side_effects=True),
        name="gather_frames")(s, st, a, at)

def exchange_kern(col_ref, row_ref, colp_ref, rowp_ref, cbuf, rbuf, csend, rsend, cgot, rgot):
    row, col, x_hi, x_lo, y, z, k = place()
    rb = z*2 + k
    me_r = x_hi*8 + y*2 + x_lo
    home = x_lo == k
    cp = []
    for s in range(8):
        other = jnp.logical_or(row != s, x_lo != k)
        c = pltpu.make_async_remote_copy(src_ref=col_ref.at[s], dst_ref=cbuf.at[rb], send_sem=csend.at[s], recv_sem=cgot.at[rb], device_id=(s, me_r), device_id_type=MESH)
        pl.when(other)(c.start)
        cp.append((c, other))
    for j in range(16):
        other = jnp.logical_or(col != j, x_lo != k)
        c = pltpu.make_async_remote_copy(src_ref=row_ref.at[j], dst_ref=rbuf.at[me_r], send_sem=rsend.at[j], recv_sem=rgot.at[me_r], device_id=(rb, j), device_id_type=MESH)
        pl.when(other)(c.start)
        cp.append((c, other))
    lc = pltpu.make_async_copy(col_ref.at[row], cbuf.at[rb], cgot.at[rb])
    lr = pltpu.make_async_copy(row_ref.at[col], rbuf.at[me_r], rgot.at[me_r])
    pl.when(home)(lc.start)
    pl.when(home)(lr.start)
    for s in range(8):
        pltpu.make_async_copy(cbuf.at[s], cbuf.at[s], cgot.at[s]).wait()
    for j in range(16):
        pltpu.make_async_copy(rbuf.at[j], rbuf.at[j], rgot.at[j]).wait()
    colp_ref[...] = functools.reduce(jnp.maximum, [cbuf[s] for s in range(8)])
    rowp_ref[...] = functools.reduce(jnp.maximum, [rbuf[j] for j in range(16)])
    for c, other in cp:
        pl.when(other)(c.wait_send)

def exchange(col, row):
    return pl.pallas_call(
        exchange_kern,
        out_shape=(jax.ShapeDtypeStruct((1, 512), F32), jax.ShapeDtypeStruct((1, 128), F32)),
        in_specs=[VM, VM], out_specs=(VM, VM),
        scratch_shapes=[
            pltpu.VMEM((8, 1, 512), F32), pltpu.VMEM((16, 1, 128), F32),
            pltpu.SemaphoreType.DMA((8,)), pltpu.SemaphoreType.DMA((16,)), pltpu.SemaphoreType.DMA((8,)), pltpu.SemaphoreType.DMA((16,)),
        ],
        compiler_params=pltpu.CompilerParams(has_side_effects=True),
        name="exchange_best")(col, row)

def on_device(stream, stream_tail, archive, archive_tail):
    v, u = gather(stream, stream_tail, archive, archive_tail)
    col, row = call(v, u)
    col, row = exchange(col, row)
    return row.reshape(-1), col.reshape(-1)

def solution(mesh):
    return jax.shard_map(
        on_device, mesh=mesh,
        in_specs=(P(("row", "col"), None), P(), P(("col", "row"), None), P()),
        out_specs=(P(("row", "col")), P(("col", "row"))),
        check_vma=False)
```

```python
import functools

import jax
import jax.numpy as jnp
from jax import lax
from jax.sharding import PartitionSpec as P
from jax.experimental import pallas as pl
from jax.experimental.pallas import tpu as pltpu

M=32; C=17; SEG=512; T=544; TV=512; NB=17; BR=384
NEG=-64.0
DN = (((1,), (0,)), ((), ()))
DT = (((1,), (1,)), ((), ()))
def split(x):
    hi = x.astype(jnp.bfloat16)
    return hi, (x - hi.astype(jnp.float32)).astype(jnp.bfloat16)
def prep_rhs(u_ref, b_ref):
    def one(c, _):
        for a in range(8):
            x = [[u_ref.at[p][pl.ds(c + 34*a + 17*h, 8, stride=272), :] for p in range(2)] for h in range(2)]
            for w in range(3):
                y = jnp.concatenate([jnp.concatenate(x[h], axis=1) for h in range(2)], axis=0)
                hi, lo = split(y)
                r = pl.multiple_of(c*BR + 16*(a + 8*w), 16)
                b_ref[pl.ds(r, 16), 0:256] = hi
                b_ref[pl.ds(r, 16), 256:512] = lo
                b_ref[pl.ds(r, 16), 512:768] = hi
                if w < 2:
                    x = [[pltpu.roll(t, 7, 0) for t in row] for row in x]
        return 0
    lax.fori_loop(0, C, one, 0)
def prep_lhs(v_ref, a_ref, t0, nt, unroll=8):
    def one(i, _):
        t = t0 + i*2
        x = jnp.concatenate([jnp.concatenate([v_ref.at[p][pl.ds(t + d, 8, stride=SEG), :] for p in range(2)], axis=1) for d in range(2)], axis=0)
        hi, lo = split(x)
        r = pl.multiple_of(t*8, 16)
        a_ref[pl.ds(r, 16), 0:256] = hi
        a_ref[pl.ds(r, 16), 256:512] = hi
        a_ref[pl.ds(r, 16), 512:768] = lo
        return 0
    lax.fori_loop(0, nt//2, one, 0, unroll=unroll)
def mm(a_ref, b_ref, g_ref, n):
    a = a_ref.at[pl.ds(pl.multiple_of(n*256, 256), 256), :]
    def rows(c):
        return b_ref[pl.ds(pl.multiple_of(c*BR + n*16, 16), 128), :]
    for j in range(9):
        cs = [2*j, 2*j+1] if j < 8 else [16]
        b = jnp.concatenate([rows(c) for c in cs], axis=0)
        g_ref[:, cs[0]*128:(cs[-1]+1)*128] = lax.dot_general(a[...], b, DT, preferred_element_type=jnp.float32)
def seg_of(lane, n):
    return (2*n + 2*(lane >> 4) + ((lane >> 3) & 1) + 16*(lane & 7)) & 127
def lane_of(seg):
    s = seg & 127
    return ((s & 15) >> 1)*16 + (s & 1)*8 + (s >> 4)
def take(x, idx):
    return jnp.take_along_axis(x, idx, axis=1)
def vblock(cur, prev, n, E, R, tm_ref, lo, hi):
    lane = lax.broadcasted_iota(jnp.int32, (8,128), 1)
    rel = seg_of(lane, 0)
    prv1, nxt1, nxt2 = lane_of(rel + 127), lane_of(rel + 1), lane_of(rel + 2)
    sg = seg_of(lane, n)
    keepx = (sg >= 2) & (sg <= 121)
    keepb = (sg >= 2) & (sg <= 122)
    keepc = (sg >= 1) & (sg <= 121)
    neg = jnp.float32(NEG)
    E = [take(e, nxt2) for e in E]
    R = [take(r, nxt2) for r in R]
    for k in range(32):
        g = lambda ref, c: ref[k*8:k*8+8, c*128:(c+1)*128]
        N = []
        for c in range(C):
            old = g(prev, c+2) if c < 15 else take(g(prev, c-15), nxt1)
            ep = E[c-1] if c else take(E[C-1], prv1)
            N.append(ep + (g(cur, c) - old))
        E = N
        if lo <= k < hi:
            R = [jnp.maximum(r, e) for r, e in zip(R, E)]
            mx = functools.reduce(jnp.maximum, E[5:14])
            mb = functools.reduce(jnp.maximum, E[0:5])
            mc = functools.reduce(jnp.maximum, E[14:17])
            m = jnp.maximum(jnp.where(keepx, mx, neg), jnp.maximum(jnp.where(keepb, mb, neg), jnp.where(keepc, mc, neg)))
            row = (n*32 + k - 31)*8
            tm_ref[pl.ds(pl.multiple_of(row, 8), 8), :] = m
    return E, R
def compute(a_ref, b_ref, gs, tm_ref):
    z = jnp.zeros((8,128), jnp.float32)
    E=[z]*C; R=[jnp.full((8,128), NEG, jnp.float32)]*C
    gs[2][...] = jnp.zeros(gs[2].shape, jnp.float32)
    mm(a_ref, b_ref, gs[0], 0)
    mm(a_ref, b_ref, gs[1], 1)
    E, R = vblock(gs[0], gs[2], 0, E, R, tm_ref, 31, 32)
    def three(m, carry):
        E, R = list(carry[0]), list(carry[1])
        for r in range(3):
            n = 1 + 3*m + r
            mm(a_ref, b_ref, gs[(2+r)%3], n+1)
            E, R = vblock(gs[(1+r)%3], gs[r%3], n, E, R, tm_ref, 0, 32)
        return tuple(E), tuple(R)
    E, R = lax.fori_loop(0, 5, three, (tuple(E), tuple(R)))
    E, R = vblock(gs[1], gs[0], 16, list(E), list(R), tm_ref, 0, 31)
    lane = lax.broadcasted_iota(jnp.int32, (8,128), 1)
    back = lane_of(lane - 32)
    return [take(r, back) for r in R]
def finish(tm_ref, R, col_ref, row_ref):
    def one(s, _):
        for tb in range(4):
            x = tm_ref[pl.ds(s + tb*1024, 128, stride=8), :]
            col_ref[s, 0:1, tb*128:(tb+1)*128] = jnp.max(x.T, axis=0, keepdims=True)*(1.0/M)
        return 0
    lax.fori_loop(0, 8, one, 0)
    rows = jnp.concatenate([jnp.max(r, axis=0, keepdims=True) for r in R] + [jnp.full((7, 128), NEG, jnp.float32)], axis=0)*(1.0/M)
    for j in range(4):
        q = lax.broadcasted_iota(jnp.int32, (128, 512), 1) + (31 + 512*j)
        pick = (lax.broadcasted_iota(jnp.int32, (128, 512), 0) == ((q*3856) >> 16)).astype(jnp.float32)
        x = lax.dot_general(rows, pick, DN, precision=lax.Precision.HIGHEST, preferred_element_type=jnp.float32)
        q = lax.broadcasted_iota(jnp.int32, (24, 512), 1) + (31 + 512*j)
        lane = (q*3856) >> 16
        x = jnp.where(lax.broadcasted_iota(jnp.int32, (24, 512), 0) == q - lane*C, x, 0.0)
        x = jnp.sum(x, axis=0, keepdims=True)
        for m in range(4):
            row_ref[4*j + m, 0:1, :] = x[:, 128*m:128*(m+1)]
def kern(v_ref, u_ref, col_ref, row_ref, a, b, g0, g1, g2, tm):
    prep_rhs(u_ref, b)
    prep_lhs(v_ref, a, 0, T)
    R = compute(a, b, [g0, g1, g2], tm)
    finish(tm, R, col_ref, row_ref)

VM = pl.BlockSpec(memory_space=pltpu.VMEM)
ANY = pl.BlockSpec(memory_space=pl.ANY)
F32 = jnp.float32

def call(v, u):
    return pl.pallas_call(
        kern,
        out_shape=(jax.ShapeDtypeStruct((8, 1, 512), F32), jax.ShapeDtypeStruct((16, 1, 128), F32)),
        in_specs=[VM, VM], out_specs=(VM, VM),
        scratch_shapes=[
            pltpu.VMEM((T*8, 768), jnp.bfloat16),
            pltpu.VMEM((C*BR, 768), jnp.bfloat16),
            pltpu.VMEM((256, C*128), F32), pltpu.VMEM((256, C*128), F32), pltpu.VMEM((256, C*128), F32),
            pltpu.VMEM((TV*8, 128), F32),
        ],
        compiler_params=pltpu.CompilerParams(vmem_limit_bytes=67043328),
        name="profile_tile")(v, u)

MESH = pl.DeviceIdType.MESH

def place():
    row, col = lax.axis_index("row"), lax.axis_index("col")
    z, x_lo = row // 2, row % 2
    x_hi, y, k = col // 8, (col // 2) % 4, col % 2
    return row, col, x_hi, x_lo, y, z, k

def dev(x, y, z, k):
    return (z*2 + x % 2, (x // 2)*8 + y*2 + k)

def unit(x):
    return x / jnp.sqrt(jnp.sum(x*x, axis=1, keepdims=True) + 1e-06)

def put_planes(dst, x):
    dst[0] = x[:, :128]
    dst[1] = x[:, 128:]

NQ = 4
CH = 512 // NQ

def gather_kern(s_ref, st_ref, a_ref, at_ref, v_ref, u_ref, su, av, tails, zeros, send, got_v, got_u, misc):
    row, col, x_hi, x_lo, y, z, k = place()
    x = x_hi*2 + x_lo
    waits = []
    count = [0]

    def remote(src, dst, sem, to, when=None):
        c = pltpu.make_async_remote_copy(src_ref=src, dst_ref=dst, send_sem=send.at[count[0]], recv_sem=sem, device_id=to, device_id_type=MESH)
        count[0] += 1
        waits.append((c, when))
        if when is None:
            c.start()
        else:
            pl.when(when)(c.start)

    def arrived(ref, sem):
        pltpu.make_async_copy(ref, ref, sem).wait()

    def vs(b, q):
        return v_ref.at[:, pl.ds(pl.multiple_of(b*512 + q*CH, CH), CH), :]

    def us(b):
        return u_ref.at[:, pl.ds(pl.multiple_of(b*128, 128), 128), :]

    put_planes(av, unit(a_ref[...]))
    put_planes(su, unit(s_ref[...]))
    zero = jnp.zeros((1, 256), F32)
    put_planes(tails.at[0], jnp.concatenate([unit(st_ref[...]), zero], axis=0))
    put_planes(tails.at[1], jnp.concatenate([unit(at_ref[...]), zero], axis=0))
    zeros[...] = jnp.zeros(zeros.shape, F32)
    home = x_lo == k
    away = x_lo != k
    for q in range(NQ):
        src = av.at[:, pl.ds(q*CH, CH), :]
        local = pltpu.make_async_copy(src, vs(row, q), got_v.at[row, q])
        pl.when(home)(local.start)
        remote(src, vs(row, q), got_v.at[row, q], dev(x_hi*2 + k, y, z, 1 - k), away)
    own = pltpu.make_async_copy(su, us(col), got_u.at[col])
    pl.when(home)(own.start)
    remote(su, us(col), got_u.at[col], dev(x, y, z, 1 - k), away)
    for p in (1, 3, 2):
        remote(su, us(col), got_u.at[col], dev((x + p*k) % 4, (y + p*(1 - k)) % 4, z, x_lo))
    pad = pltpu.make_async_copy(zeros, u_ref.at[:, pl.ds(2080, 96), :], misc.at[0])
    pad.start()
    bo = z*2 + k
    up, dn, far = (z + 1) % 4, (z + 3) % 4, (z + 2) % 4
    for q in range(NQ):
        arrived(vs(bo, q), got_v.at[bo, q])
        remote(vs(bo, q), vs(bo, q), got_v.at[bo, q], dev(x, y, up, k))
        remote(vs(bo, q), vs(bo, q), got_v.at[bo, q], dev(x, y, dn, k))
        remote(vs(bo, q), vs(bo, q), got_v.at[bo, q], dev(x, y, z, 1 - k))
    for xs in range(2):
        b = xs*8 + y*2 + 1
        arrived(us(b), got_u.at[b])
        for p in (1, 3, 2):
            remote(us(b), us(b), got_u.at[b], dev(x, (y + p) % 4, z, k))
    for yy in range(4):
        b = x_hi*8 + yy*2
        pl.when(home)(lambda b=b: arrived(us(b), got_u.at[b]))
        for p in (1, 3, 2):
            remote(us(b), us(b), got_u.at[b], dev((x + p) % 4, y, z, k), home)
    bu, bd, bf = up*2 + k, dn*2 + k, far*2 + k
    for q in range(NQ):
        arrived(vs(bd, q), got_v.at[bd, q])
        if q % 2 == 0:
            remote(vs(bd, q), vs(bd, q), got_v.at[bd, q], dev(x, y, up, k))
        remote(vs(bd, q), vs(bd, q), got_v.at[bd, q], dev(x, y, z, 1 - k))
        arrived(vs(bu, q), got_v.at[bu, q])
        if q % 2 == 1:
            remote(vs(bu, q), vs(bu, q), got_v.at[bu, q], dev(x, y, dn, k))
        remote(vs(bu, q), vs(bu, q), got_v.at[bu, q], dev(x, y, z, 1 - k))
    for q in range(NQ):
        arrived(vs(bf, q), got_v.at[bf, q])
        remote(vs(bf, q), vs(bf, q), got_v.at[bf, q], dev(x, y, z, 1 - k))
    for zz in range(4):
        for q in range(NQ):
            b = zz*2 + 1 - k
            arrived(vs(b, q), got_v.at[b, q])
    for xs in range(2):
        for yy in range(4):
            b = xs*8 + yy*2 + 1
            pl.when(yy != y)(lambda b=b: arrived(us(b), got_u.at[b]))
            b = xs*8 + yy*2
            pl.when(jnp.logical_or(away, xs != x_hi))(lambda b=b: arrived(us(b), got_u.at[b]))
    cb = (x_hi*4 + y)*2 + x_lo
    pc = (cb + 15) % 16
    rb = z*2 + k
    pr = (rb + 7) % 8
    remote(v_ref.at[:, pl.ds(0, 32), :], v_ref.at[:, pl.ds(4096, 32), :], misc.at[1], dev((pc // 8)*2 + pc % 2, (pc // 2) % 4, z, k), cb != 0)
    remote(u_ref.at[:, pl.ds(0, 32), :], u_ref.at[:, pl.ds(2048, 32), :], misc.at[2], dev(x, y, pr // 2, pr % 2), rb != 0)
    tv = pltpu.make_async_copy(tails.at[1], v_ref.at[:, pl.ds(4096, 32), :], misc.at[1])
    tu = pltpu.make_async_copy(tails.at[0], u_ref.at[:, pl.ds(2048, 32), :], misc.at[2])
    pl.when(cb == 15)(tv.start)
    pl.when(rb == 7)(tu.start)
    tv.wait()
    tu.wait()
    pad.wait()
    for c, when in waits:
        if when is None:
            c.wait_send()
        else:
            pl.when(when)(c.wait_send)

def gather(s, st, a, at):
    return pl.pallas_call(
        gather_kern,
        out_shape=(jax.ShapeDtypeStruct((2, 4128, 128), F32), jax.ShapeDtypeStruct((2, 2176, 128), F32)),
        in_specs=[VM]*4, out_specs=(ANY, ANY),
        scratch_shapes=[
            pltpu.VMEM((2, 128, 128), F32), pltpu.VMEM((2, 512, 128), F32),
            pltpu.VMEM((2, 2, 32, 128), F32), pltpu.VMEM((2, 96, 128), F32),
            pltpu.SemaphoreType.DMA((72,)), pltpu.SemaphoreType.DMA((8, NQ)), pltpu.SemaphoreType.DMA((16,)), pltpu.SemaphoreType.DMA((3,)),
        ],
        compiler_params=pltpu.CompilerParams(has_side_effects=True),
        name="gather_frames")(s, st, a, at)

def exchange_kern(col_ref, row_ref, colp_ref, rowp_ref, cbuf, rbuf, csend, rsend, cgot, rgot):
    row, col, x_hi, x_lo, y, z, k = place()
    rb = z*2 + k
    me_r = x_hi*8 + y*2 + x_lo
    home = x_lo == k
    cp = []
    for s in range(8):
        other = jnp.logical_or(row != s, x_lo != k)
        c = pltpu.make_async_remote_copy(src_ref=col_ref.at[s], dst_ref=cbuf.at[rb], send_sem=csend.at[s], recv_sem=cgot.at[rb], device_id=(s, me_r), device_id_type=MESH)
        pl.when(other)(c.start)
        cp.append((c, other))
    for j in range(16):
        other = jnp.logical_or(col != j, x_lo != k)
        c = pltpu.make_async_remote_copy(src_ref=row_ref.at[j], dst_ref=rbuf.at[me_r], send_sem=rsend.at[j], recv_sem=rgot.at[me_r], device_id=(rb, j), device_id_type=MESH)
        pl.when(other)(c.start)
        cp.append((c, other))
    lc = pltpu.make_async_copy(col_ref.at[row], cbuf.at[rb], cgot.at[rb])
    lr = pltpu.make_async_copy(row_ref.at[col], rbuf.at[me_r], rgot.at[me_r])
    pl.when(home)(lc.start)
    pl.when(home)(lr.start)
    for s in range(8):
        pltpu.make_async_copy(cbuf.at[s], cbuf.at[s], cgot.at[s]).wait()
    for j in range(16):
        pltpu.make_async_copy(rbuf.at[j], rbuf.at[j], rgot.at[j]).wait()
    colp_ref[...] = functools.reduce(jnp.maximum, [cbuf[s] for s in range(8)])
    rowp_ref[...] = functools.reduce(jnp.maximum, [rbuf[j] for j in range(16)])
    for c, other in cp:
        pl.when(other)(c.wait_send)

def exchange(col, row):
    return pl.pallas_call(
        exchange_kern,
        out_shape=(jax.ShapeDtypeStruct((1, 512), F32), jax.ShapeDtypeStruct((1, 128), F32)),
        in_specs=[VM, VM], out_specs=(VM, VM),
        scratch_shapes=[
            pltpu.VMEM((8, 1, 512), F32), pltpu.VMEM((16, 1, 128), F32),
            pltpu.SemaphoreType.DMA((8,)), pltpu.SemaphoreType.DMA((16,)), pltpu.SemaphoreType.DMA((8,)), pltpu.SemaphoreType.DMA((16,)),
        ],
        compiler_params=pltpu.CompilerParams(has_side_effects=True),
        name="exchange_best")(col, row)

def on_device(stream, stream_tail, archive, archive_tail):
    v, u = gather(stream, stream_tail, archive, archive_tail)
    col, row = call(v, u)
    col, row = exchange(col, row)
    return row.reshape(-1), col.reshape(-1)

def solution(mesh):
    return jax.shard_map(
        on_device, mesh=mesh,
        in_specs=(P(("row", "col"), None), P(), P(("col", "row"), None), P()),
        out_specs=(P(("row", "col")), P(("col", "row"))),
        check_vma=False)
```

```python
import functools

import jax
import jax.numpy as jnp
from jax import lax
from jax.sharding import PartitionSpec as P
from jax.experimental import pallas as pl
from jax.experimental.pallas import tpu as pltpu

M=32; C=17; SEG=512; T=544; TV=512; NB=17; BR=384
NEG=-64.0
DN = (((1,), (0,)), ((), ()))
DT = (((1,), (1,)), ((), ()))
def split(x):
    hi = x.astype(jnp.bfloat16)
    return hi, (x - hi.astype(jnp.float32)).astype(jnp.bfloat16)
def prep_rhs(u_ref, b_ref):
    def one(c, _):
        for a in range(8):
            x = [[u_ref.at[p][pl.ds(c + 34*a + 17*h, 8, stride=272), :] for p in range(2)] for h in range(2)]
            for w in range(3):
                y = jnp.concatenate([jnp.concatenate(x[h], axis=1) for h in range(2)], axis=0)
                hi, lo = split(y)
                r = pl.multiple_of(c*BR + 16*(a + 8*w), 16)
                b_ref[pl.ds(r, 16), 0:256] = hi
                b_ref[pl.ds(r, 16), 256:512] = lo
                b_ref[pl.ds(r, 16), 512:768] = hi
                if w < 2:
                    x = [[pltpu.roll(t, 7, 0) for t in row] for row in x]
        return 0
    lax.fori_loop(0, C, one, 0)
def prep_lhs(v_ref, a_ref, t0, nt, unroll=8):
    def one(i, _):
        t = t0 + i*2
        x = jnp.concatenate([jnp.concatenate([v_ref.at[p][pl.ds(t + d, 8, stride=SEG), :] for p in range(2)], axis=1) for d in range(2)], axis=0)
        hi, lo = split(x)
        r = pl.multiple_of(t*8, 16)
        a_ref[pl.ds(r, 16), 0:256] = hi
        a_ref[pl.ds(r, 16), 256:512] = hi
        a_ref[pl.ds(r, 16), 512:768] = lo
        return 0
    lax.fori_loop(0, nt//2, one, 0, unroll=unroll)
def mm(a_ref, b_ref, g_ref, n):
    a = a_ref.at[pl.ds(pl.multiple_of(n*256, 256), 256), :]
    def rows(c):
        return b_ref[pl.ds(pl.multiple_of(c*BR + n*16, 16), 128), :]
    for j in range(9):
        cs = [2*j, 2*j+1] if j < 8 else [16]
        b = jnp.concatenate([rows(c) for c in cs], axis=0)
        g_ref[:, cs[0]*128:(cs[-1]+1)*128] = lax.dot_general(a[...], b, DT, preferred_element_type=jnp.float32)
def seg_of(lane, n):
    return (2*n + 2*(lane >> 4) + ((lane >> 3) & 1) + 16*(lane & 7)) & 127
def lane_of(seg):
    s = seg & 127
    return ((s & 15) >> 1)*16 + (s & 1)*8 + (s >> 4)
def take(x, idx):
    return jnp.take_along_axis(x, idx, axis=1)
def vblock(cur, prev, n, E, R, tm_ref, lo, hi):
    lane = lax.broadcasted_iota(jnp.int32, (8,128), 1)
    rel = seg_of(lane, 0)
    prv1, nxt1, nxt2 = lane_of(rel + 127), lane_of(rel + 1), lane_of(rel + 2)
    sg = seg_of(lane, n)
    keepx = (sg >= 2) & (sg <= 121)
    keepb = (sg >= 2) & (sg <= 122)
    keepc = (sg >= 1) & (sg <= 121)
    neg = jnp.float32(NEG)
    E = [take(e, nxt2) for e in E]
    R = [take(r, nxt2) for r in R]
    for k in range(32):
        g = lambda ref, c: ref[k*8:k*8+8, c*128:(c+1)*128]
        N = []
        for c in range(C):
            old = g(prev, c+2) if c < 15 else take(g(prev, c-15), nxt1)
            ep = E[c-1] if c else take(E[C-1], prv1)
            N.append(ep + (g(cur, c) - old))
        E = N
        if lo <= k < hi:
            R = [jnp.maximum(r, e) for r, e in zip(R, E)]
            mx = functools.reduce(jnp.maximum, E[5:14])
            mb = functools.reduce(jnp.maximum, E[0:5])
            mc = functools.reduce(jnp.maximum, E[14:17])
            m = jnp.maximum(jnp.where(keepx, mx, neg), jnp.maximum(jnp.where(keepb, mb, neg), jnp.where(keepc, mc, neg)))
            row = (n*32 + k - 31)*8
            tm_ref[pl.ds(pl.multiple_of(row, 8), 8), :] = m
    return E, R
def compute(a_ref, b_ref, gs, tm_ref, service):
    z = jnp.zeros((8,128), jnp.float32)
    E=[z]*C; R=[jnp.full((8,128), NEG, jnp.float32)]*C
    gs[2][...] = jnp.zeros(gs[2].shape, jnp.float32)
    mm(a_ref, b_ref, gs[0], 0)
    mm(a_ref, b_ref, gs[1], 1)
    E, R = vblock(gs[0], gs[2], 0, E, R, tm_ref, 31, 32)
    def three(m, carry):
        E, R = list(carry[0]), list(carry[1])
        service(m)
        for r in range(3):
            n = 1 + 3*m + r
            mm(a_ref, b_ref, gs[(2+r)%3], n+1)
            E, R = vblock(gs[(1+r)%3], gs[r%3], n, E, R, tm_ref, 0, 32)
        return tuple(E), tuple(R)
    E, R = lax.fori_loop(0, 5, three, (tuple(E), tuple(R)))
    E, R = vblock(gs[1], gs[0], 16, list(E), list(R), tm_ref, 0, 31)
    lane = lax.broadcasted_iota(jnp.int32, (8,128), 1)
    back = lane_of(lane - 32)
    return [take(r, back) for r in R]
def finish(tm_ref, R, col_ref, row_ref):
    def one(s, _):
        for tb in range(4):
            x = tm_ref[pl.ds(s + tb*1024, 128, stride=8), :]
            col_ref[s, 0:1, tb*128:(tb+1)*128] = jnp.max(x.T, axis=0, keepdims=True)*(1.0/M)
        return 0
    lax.fori_loop(0, 8, one, 0)
    rows = jnp.concatenate([jnp.max(r, axis=0, keepdims=True) for r in R] + [jnp.full((7, 128), NEG, jnp.float32)], axis=0)*(1.0/M)
    for j in range(4):
        q = lax.broadcasted_iota(jnp.int32, (128, 512), 1) + (31 + 512*j)
        pick = (lax.broadcasted_iota(jnp.int32, (128, 512), 0) == ((q*3856) >> 16)).astype(jnp.float32)
        x = lax.dot_general(rows, pick, DN, precision=lax.Precision.HIGHEST, preferred_element_type=jnp.float32)
        q = lax.broadcasted_iota(jnp.int32, (24, 512), 1) + (31 + 512*j)
        lane = (q*3856) >> 16
        x = jnp.where(lax.broadcasted_iota(jnp.int32, (24, 512), 0) == q - lane*C, x, 0.0)
        x = jnp.sum(x, axis=0, keepdims=True)
        for m in range(4):
            row_ref[4*j + m, 0:1, :] = x[:, 128*m:128*(m+1)]
VM = pl.BlockSpec(memory_space=pltpu.VMEM)
F32 = jnp.float32
MESH = pl.DeviceIdType.MESH
NQ = 4
CH = 512 // NQ

def dev(x, y, z, k):
    return (z*2 + x % 2, (x // 2)*8 + y*2 + k)

def unit(x):
    return x / jnp.sqrt(jnp.sum(x*x, axis=1, keepdims=True) + 1e-06)

def put_planes(dst, x):
    dst[0] = x[:, :128]
    dst[1] = x[:, 128:]

def kern(s_ref, st_ref, a_ref, at_ref, colp_ref, rowp_ref, v_ref, u_ref, su, av, tails, a3, bt, g0, g1, g2, tm,
         colm, rowm, cbuf, rbuf, send, got_v, got_u, misc, csend, rsend, cgot, rgot):
    row, col = lax.axis_index("row"), lax.axis_index("col")
    z, x_lo = row // 2, row % 2
    x_hi, y, k = col // 8, (col // 2) % 4, col % 2
    x = x_hi*2 + x_lo
    home = x_lo == k
    away = x_lo != k
    cb = (x_hi*4 + y)*2 + x_lo
    rb = z*2 + k
    me_r = x_hi*8 + y*2 + x_lo
    pc, nc = (cb + 15) % 16, (cb + 1) % 16
    pr = (rb + 7) % 8
    waits, later = [], []
    count = [0]

    def remote(src, dst, sem, to, when=None, guard=None):
        c = pltpu.make_async_remote_copy(src_ref=src, dst_ref=dst, send_sem=send.at[count[0]], recv_sem=sem, device_id=to, device_id_type=MESH)
        index = count[0]
        count[0] += 1
        if guard is None:
            waits.append((c, when))
        else:
            later.append((index,) + guard)
        if when is None:
            c.start()
        else:
            pl.when(when)(c.start)

    def arrived(ref, sem):
        pltpu.make_async_copy(ref, ref, sem).wait()

    def vs(b, q):
        return v_ref.at[:, pl.ds(pl.multiple_of(b*512 + q*CH, CH), CH), :]

    def us(b, h):
        return u_ref.at[:, pl.ds(pl.multiple_of(b*128 + h*64, 64), 64), :]

    bar = pltpu.get_barrier_semaphore()

    def hello(to):
        pl.semaphore_signal(bar, inc=1, device_id=to, device_id_type=MESH)

    for c in range(2):
        for p in (1, 2, 3):
            hello(dev((x + p) % 4, y, z, c))
            hello(dev(x, (y + p) % 4, z, c))
            hello(dev(x, y, (z + p) % 4, c))
    hello(dev(x, y, z, 1 - k))
    for o in (pc, nc):
        hello(dev((o // 8)*2 + o % 2, (o // 2) % 4, z, k))
    for xx in range(4):
        for yy in range(4):
            pl.when(jnp.logical_or(away, jnp.logical_or(x != xx, y != yy)))(lambda xx=xx, yy=yy: hello(dev(xx, yy, z, x_lo)))
    for zz in range(4):
        for c in range(2):
            pl.when(jnp.logical_or(away, jnp.logical_or(z != zz, k != c)))(lambda zz=zz, c=c: hello(dev(x_hi*2 + k, y, zz, c)))

    put_planes(su, unit(s_ref[...]))
    put_planes(av, unit(a_ref[...]))
    zero = jnp.zeros((1, 256), F32)
    put_planes(tails.at[0], jnp.concatenate([unit(st_ref[...]), zero], axis=0))
    put_planes(tails.at[1], jnp.concatenate([unit(at_ref[...]), zero], axis=0))
    u_ref[:, 2080:2176, :] = jnp.zeros((2, 96, 128), F32)
    pl.when(home)(lambda: pl.semaphore_wait(bar, 43))
    pl.when(away)(lambda: pl.semaphore_wait(bar, 45))

    for h in range(2):
        src = su.at[:, pl.ds(h*64, 64), :]
        own = pltpu.make_async_copy(src, us(col, h), got_u.at[col, h])
        pl.when(home)(own.start)
        remote(src, us(col, h), got_u.at[col, h], dev(x, y, z, 1 - k), away)
        for p in (1, 3):
            remote(src, us(col, h), got_u.at[col, h], dev((x + p*k) % 4, (y + p*(1 - k)) % 4, z, x_lo))
    for q in range(NQ):
        src = av.at[:, pl.ds(q*CH, CH), :]
        local = pltpu.make_async_copy(src, vs(row, q), got_v.at[row, q])
        pl.when(home)(local.start)
        remote(src, vs(row, q), got_v.at[row, q], dev(x_hi*2 + k, y, z, 1 - k), away)
    bo = z*2 + k
    up, dn, far = (z + 1) % 4, (z + 3) % 4, (z + 2) % 4

    def ring(q):
        arrived(vs(bo, q), got_v.at[bo, q])
        for to in (dev(x, y, up, k), dev(x, y, dn, k), dev(x, y, z, 1 - k)):
            remote(vs(bo, q), vs(bo, q), got_v.at[bo, q], to)

    ring(0)
    ring(1)
    base = count[0]
    top = [0]

    def stream(flag, cols, steps):
        count[0] = base

        def blk(c, xc, dy):
            return (cols[xc] // 2)*8 + ((y + dy) % 4)*2 + c

        def get(c, xc, dy):
            b = blk(c, xc, dy)
            for h in range(2):
                arrived(us(b, h), got_u.at[b, h])

        def put(c, xc, dy, hs, to):
            b = blk(c, xc, dy)
            for h in hs:
                remote(us(b, h), us(b, h), got_u.at[b, h], to, guard=(0, flag))

        pl.when(flag)(lambda: steps(get, put))
        top[0] = max(top[0], count[0])

    def dx(p):
        return dev((x + p) % 4, y, z, k)

    def dy_(p):
        return dev(x, (y + p) % 4, z, k)

    def both(c, xc, d, to):
        return [(c, xc, d, (0, 1), t) for t in to]

    def home_steps(get, put):
        alongx, alongy = (dx(1), dx(3)), (dy_(1), dy_(3))
        for c, to in ((0, alongx), (1, alongy)):
            get(c, 0, 0)
            for o in both(c, 0, 0, to):
                put(*o)
        get(0, 0, 3)
        put(0, 0, 3, (0,), dy_(1))
        for o in both(0, 0, 3, alongx):
            put(*o)
        get(0, 0, 1)
        put(0, 0, 1, (1,), dy_(3))
        for o in both(0, 0, 1, alongx):
            put(*o)
        get(1, 1, 0)
        for o in both(1, 1, 0, alongy):
            put(*o)
        get(0, 0, 2)
        for o in both(0, 0, 2, alongx):
            put(*o)
        for xc in range(2):
            get(1, xc, 3)
            put(1, xc, 3, (0,), dy_(1))
            get(1, xc, 1)
            put(1, xc, 1, (1,), dy_(3))
        for xc in range(2):
            get(1, xc, 2)
        for d in range(4):
            get(0, 1, d)

    def away_steps(get, put):
        alongy = (dy_(1), dy_(3))
        get(1, 0, 0)
        put(1, 0, 0, (0,), dx(1))
        for o in both(1, 0, 0, alongy):
            put(*o)
        get(1, 1, 0)
        put(1, 1, 0, (1,), dx(3))
        for o in both(1, 1, 0, alongy):
            put(*o)

        def relay(d):
            get(0, 0, d)
            put(0, 0, d, (0,), dx(1))
            get(0, 1, d)
            put(0, 1, d, (1,), dx(3))

        relay(0)
        for xc in range(2):
            get(1, xc, 3)
            put(1, xc, 3, (0,), dy_(1))
            get(1, xc, 1)
            put(1, xc, 1, (1,), dy_(3))
        relay(3)
        relay(1)
        relay(2)
        for xc in range(2):
            get(1, xc, 2)

    stream(home, (x, (x + 2) % 4), home_steps)
    stream(away, ((x + 3) % 4, (x + 1) % 4), away_steps)
    count[0] = top[0]
    ring(2)
    ring(3)
    remote(u_ref.at[:, pl.ds(0, 32), :], u_ref.at[:, pl.ds(2048, 32), :], misc.at[0], dev(x, y, pr // 2, pr % 2), rb != 0)
    tu = pltpu.make_async_copy(tails.at[0], u_ref.at[:, pl.ds(2048, 32), :], misc.at[0])
    pl.when(rb == 7)(tu.start)
    bu, bd, bf = up*2 + k, dn*2 + k, far*2 + k

    def near(q):
        for b, to, turn in ((bd, up, 0), (bu, dn, 1)):
            arrived(vs(b, q), got_v.at[b, q])
            if q % 2 == turn:
                remote(vs(b, q), vs(b, q), got_v.at[b, q], dev(x, y, to, k))
            remote(vs(b, q), vs(b, q), got_v.at[b, q], dev(x, y, z, 1 - k))

    def distant(q):
        arrived(vs(bf, q), got_v.at[bf, q])
        remote(vs(bf, q), vs(bf, q), got_v.at[bf, q], dev(x, y, z, 1 - k), guard=(0,))

    def others(q):
        for zz in range(4):
            b = zz*2 + 1 - k
            arrived(vs(b, q), got_v.at[b, q])

    for q in range(NQ):
        near(q)
    tu.wait()
    prep_rhs(u_ref, bt)
    distant(0)
    distant(1)
    others(0)
    remote(v_ref.at[:, pl.ds(0, 32), :], v_ref.at[:, pl.ds(4096, 32), :], misc.at[1], dev((pc // 8)*2 + pc % 2, (pc // 2) % 4, z, k), cb != 0)
    tv = pltpu.make_async_copy(tails.at[1], v_ref.at[:, pl.ds(4096, 32), :], misc.at[1])
    pl.when(cb == 15)(tv.start)
    others(1)
    prep_lhs(v_ref, a3, 0, 256)

    def service(m):
        def early():
            distant(2)
            distant(3)

        def third():
            others(2)
            prep_lhs(v_ref, a3, 256, 128)

        def fourth():
            others(3)
            prep_lhs(v_ref, a3, 384, 128)

        def last():
            tv.wait()
            prep_lhs(v_ref, a3, 512, 32)

        pl.when(m == 1)(early)
        pl.when(m == 2)(third)
        pl.when(m == 3)(fourth)
        pl.when(m == 4)(last)

    R = compute(a3, bt, [g0, g1, g2], tm, service)
    finish(tm, R, colm, rowm)
    for c, when in waits:
        if when is None:
            c.wait_send()
        else:
            pl.when(when)(c.wait_send)
    for index, *how in later:
        if len(how) == 1:
            arrived(vs(0, 0), send.at[index])
        else:
            pl.when(how[1])(lambda index=index: arrived(us(0, 0), send.at[index]))
    cp = []
    for s in range(8):
        other = jnp.logical_or(row != s, away)
        c = pltpu.make_async_remote_copy(src_ref=colm.at[s], dst_ref=cbuf.at[rb], send_sem=csend.at[s], recv_sem=cgot.at[rb], device_id=(s, me_r), device_id_type=MESH)
        pl.when(other)(c.start)
        cp.append((c, other))
    for j in range(16):
        other = jnp.logical_or(col != j, away)
        c = pltpu.make_async_remote_copy(src_ref=rowm.at[j], dst_ref=rbuf.at[me_r], send_sem=rsend.at[j], recv_sem=rgot.at[me_r], device_id=(rb, j), device_id_type=MESH)
        pl.when(other)(c.start)
        cp.append((c, other))
    lc = pltpu.make_async_copy(colm.at[row], cbuf.at[rb], cgot.at[rb])
    lr = pltpu.make_async_copy(rowm.at[col], rbuf.at[me_r], rgot.at[me_r])
    pl.when(home)(lc.start)
    pl.when(home)(lr.start)
    for s in range(8):
        arrived(cbuf.at[s], cgot.at[s])
    for j in range(16):
        arrived(rbuf.at[j], rgot.at[j])
    colp_ref[...] = functools.reduce(jnp.maximum, [cbuf[s] for s in range(8)])
    rowp_ref[...] = functools.reduce(jnp.maximum, [rbuf[j] for j in range(16)])
    for c, other in cp:
        pl.when(other)(c.wait_send)

def on_device(stream, stream_tail, archive, archive_tail):
    DMA = pltpu.SemaphoreType.DMA
    col, row = pl.pallas_call(
        kern,
        out_shape=(jax.ShapeDtypeStruct((1, 512), F32), jax.ShapeDtypeStruct((1, 128), F32)),
        in_specs=[VM]*4, out_specs=(VM, VM),
        scratch_shapes=[
            pltpu.VMEM((2, 4128, 128), F32), pltpu.VMEM((2, 2176, 128), F32),
            pltpu.VMEM((2, 128, 128), F32), pltpu.VMEM((2, 512, 128), F32), pltpu.VMEM((2, 2, 32, 128), F32),
            pltpu.VMEM((T*8, 768), jnp.bfloat16), pltpu.VMEM((C*BR, 768), jnp.bfloat16),
            pltpu.VMEM((256, C*128), F32), pltpu.VMEM((256, C*128), F32), pltpu.VMEM((256, C*128), F32),
            pltpu.VMEM((TV*8, 128), F32),
            pltpu.VMEM((8, 1, 512), F32), pltpu.VMEM((16, 1, 128), F32),
            pltpu.VMEM((8, 1, 512), F32), pltpu.VMEM((16, 1, 128), F32),
            DMA((100,)), DMA((8, NQ)), DMA((16, 2)), DMA((2,)),
            DMA((8,)), DMA((16,)), DMA((8,)), DMA((16,)),
        ],
        compiler_params=pltpu.CompilerParams(has_side_effects=True, collective_id=0, vmem_limit_bytes=67043328),
        name="join_profile")(stream, stream_tail, archive, archive_tail)
    return row.reshape(-1), col.reshape(-1)

def solution(mesh):
    return jax.shard_map(
        on_device, mesh=mesh,
        in_specs=(P(("row", "col"), None), P(), P(("col", "row"), None), P()),
        out_specs=(P(("row", "col")), P(("col", "row"))),
        check_vma=False)
```

```python
import functools

import jax
import jax.numpy as jnp
from jax import lax
from jax.sharding import PartitionSpec as P
from jax.experimental import pallas as pl
from jax.experimental.pallas import tpu as pltpu

M=32; C=17; SEGR=544; T=544; TV=512; NB=17; BR=384
NEG=-64.0
DN = (((1,), (0,)), ((), ()))
DT = (((1,), (1,)), ((), ()))
def split(x):
    hi = x.astype(jnp.bfloat16)
    return hi, (x - hi.astype(jnp.float32)).astype(jnp.bfloat16)
def prep_rhs(u_ref, b_ref):
    def one(c, _):
        for a in range(8):
            x = [[u_ref.at[p][pl.ds(c + 34*a + 17*h, 8, stride=272), :] for p in range(2)] for h in range(2)]
            for w in range(3):
                y = jnp.concatenate([jnp.concatenate(x[h], axis=1) for h in range(2)], axis=0)
                hi, lo = split(y)
                r = pl.multiple_of(c*BR + 16*(a + 8*w), 16)
                b_ref[pl.ds(r, 16), 0:256] = hi
                b_ref[pl.ds(r, 16), 256:512] = lo
                b_ref[pl.ds(r, 16), 512:768] = hi
                if w < 2:
                    x = [[pltpu.roll(t, 7, 0) for t in row] for row in x]
        return 0
    lax.fori_loop(0, C, one, 0)
def prep_lhs(v_ref, a_ref, n):
    for i in range(16):
        x = jnp.concatenate([jnp.concatenate([v_ref.at[p][pl.ds(n*32 + 2*i + d, 8, stride=SEGR), :] for p in range(2)], axis=1) for d in range(2)], axis=0)
        hi, lo = split(x)
        a_ref[16*i:16*i+16, 0:256] = hi
        a_ref[16*i:16*i+16, 256:512] = hi
        a_ref[16*i:16*i+16, 512:768] = lo
def mm(a_ref, b_ref, g_ref, n):
    def rows(c):
        return b_ref[pl.ds(pl.multiple_of(c*BR + n*16, 16), 128), :]
    for j in range(9):
        cs = [2*j, 2*j+1] if j < 8 else [16]
        b = jnp.concatenate([rows(c) for c in cs], axis=0)
        g_ref[:, cs[0]*128:(cs[-1]+1)*128] = lax.dot_general(a_ref[...], b, DT, preferred_element_type=jnp.float32)
def seg_of(lane, n):
    return (2*n + 2*(lane >> 4) + ((lane >> 3) & 1) + 16*(lane & 7)) & 127
def lane_of(seg):
    s = seg & 127
    return ((s & 15) >> 1)*16 + (s & 1)*8 + (s >> 4)
def take(x, idx):
    return jnp.take_along_axis(x, idx, axis=1)
def vblock(cur, prev, n, E, R, acc_ref, lo, hi):
    lane = lax.broadcasted_iota(jnp.int32, (8,128), 1)
    rel = seg_of(lane, 0)
    prv1, nxt1, nxt2 = lane_of(rel + 127), lane_of(rel + 1), lane_of(rel + 2)
    sg = seg_of(lane, n)
    keepx = (sg >= 2) & (sg <= 121)
    keepb = (sg >= 2) & (sg <= 122)
    keepc = (sg >= 1) & (sg <= 121)
    neg = jnp.float32(NEG)
    acc = jnp.full((8, 128), NEG, jnp.float32)
    spot = (n & 3)*32
    E = [take(e, nxt2) for e in E]
    R = [take(r, nxt2) for r in R]
    for k in range(32):
        g = lambda ref, c: ref[k*8:k*8+8, c*128:(c+1)*128]
        N = []
        for c in range(C):
            old = g(prev, c+2) if c < 15 else take(g(prev, c-15), nxt1)
            ep = E[c-1] if c else take(E[C-1], prv1)
            N.append(ep + (g(cur, c) - old))
        E = N
        if lo <= k < hi:
            R = [jnp.maximum(r, e) for r, e in zip(R, E)]
            mx = functools.reduce(jnp.maximum, E[5:14])
            mb = functools.reduce(jnp.maximum, E[0:5])
            mc = functools.reduce(jnp.maximum, E[14:17])
            m = jnp.maximum(jnp.where(keepx, mx, neg), jnp.maximum(jnp.where(keepb, mb, neg), jnp.where(keepc, mc, neg)))
            acc = jnp.where(lane == spot + k, jnp.max(m, axis=1, keepdims=True), acc)
    tile = acc_ref.at[:, pl.ds(pl.multiple_of((n >> 2)*128, 128), 128)]
    tile[...] = jnp.where((lane >> 5) == (n & 3), acc, tile[...])
    return E, R
def compute(v_ref, a, b_ref, gs, acc_ref, service):
    z = jnp.zeros((8,128), jnp.float32)
    E = [z]*C
    R = [jnp.full((8,128), NEG, jnp.float32)]*C
    gs[2][...] = jnp.zeros(gs[2].shape, jnp.float32)
    first = jnp.int32(0)
    for n in range(3):
        prep_lhs(v_ref, a[n], n)
    mm(a[0], b_ref, gs[0], 0)
    mm(a[1], b_ref, gs[1], 1)
    E, R = vblock(gs[0], gs[2], first, E, R, acc_ref, 31, 32)
    def three(m, carry):
        E, R = list(carry[0]), list(carry[1])
        service(m)
        for r in range(3):
            n = 1 + 3*m + r
            mm(a[(2+r)%3], b_ref, gs[(2+r)%3], n+1)
            prep_lhs(v_ref, a[r%3], jnp.minimum(n+2, NB-1))
            E, R = vblock(gs[(1+r)%3], gs[r%3], n, E, R, acc_ref, 0, 32)
        return tuple(E), tuple(R)
    E, R = lax.fori_loop(0, 5, three, (tuple(E), tuple(R)))
    E, R = vblock(gs[1], gs[0], first + 16, list(E), list(R), acc_ref, 0, 31)
    lane = lax.broadcasted_iota(jnp.int32, (8,128), 1)
    back = lane_of(lane - 32)
    return [take(r, back) for r in R]
def finish(acc_ref, R, col_ref, row_ref):
    lane = lax.broadcasted_iota(jnp.int32, (8, 128), 1)
    turned = [pltpu.roll(acc_ref[:, 128*j:128*(j+1)], 97, 1) for j in range(5)]
    for j in range(4):
        best = jnp.where(lane < 97, turned[j], turned[j+1])*(1.0/M)
        for s in range(8):
            col_ref[s, 0:1, 128*j:128*(j+1)] = best[s:s+1]
    rows = jnp.concatenate([jnp.max(r, axis=0, keepdims=True) for r in R] + [jnp.full((7, 128), NEG, jnp.float32)], axis=0)*(1.0/M)
    for j in range(4):
        q = lax.broadcasted_iota(jnp.int32, (128, 512), 1) + (31 + 512*j)
        pick = (lax.broadcasted_iota(jnp.int32, (128, 512), 0) == ((q*3856) >> 16)).astype(jnp.float32)
        x = lax.dot_general(rows, pick, DN, precision=lax.Precision.HIGHEST, preferred_element_type=jnp.float32)
        q = lax.broadcasted_iota(jnp.int32, (24, 512), 1) + (31 + 512*j)
        lane = (q*3856) >> 16
        x = jnp.where(lax.broadcasted_iota(jnp.int32, (24, 512), 0) == q - lane*C, x, 0.0)
        x = jnp.sum(x, axis=0, keepdims=True)
        for m in range(4):
            row_ref[4*j + m, 0:1, :] = x[:, 128*m:128*(m+1)]
VM = pl.BlockSpec(memory_space=pltpu.VMEM)
F32 = jnp.float32
MESH = pl.DeviceIdType.MESH
NQ = 4
CH = SEGR // NQ

def dev(x, y, z, k):
    return (z*2 + x % 2, (x // 2)*8 + y*2 + k)

def unit(x):
    return x * (1.0 / jnp.sqrt(jnp.sum(x*x, axis=1, keepdims=True) + 1e-06))

def put_planes(dst, x):
    dst[0] = x[:, :128]
    dst[1] = x[:, 128:]

def kern(s_ref, st_ref, a_ref, at_ref, colp_ref, rowp_ref, v_ref, u_ref, su, tails, a0, a1, a2, bt, g0, g1, g2, acc,
         colm, rowm, cbuf, rbuf, send, got_v, got_u, misc, csend, rsend, cgot, rgot):
    row, col = lax.axis_index("row"), lax.axis_index("col")
    z, x_lo = row // 2, row % 2
    x_hi, y, k = col // 8, (col // 2) % 4, col % 2
    x = x_hi*2 + x_lo
    home = x_lo == k
    away = x_lo != k
    rb = z*2 + k
    me_r = x_hi*8 + y*2 + x_lo
    blk_no = col*8 + row
    pb, nb = (blk_no + 127) % 128, (blk_no + 1) % 128
    pr = (rb + 7) % 8
    waits, later = [], []
    count = [0]

    def remote(src, dst, sem, to, when=None, guard=None):
        c = pltpu.make_async_remote_copy(src_ref=src, dst_ref=dst, send_sem=send.at[count[0]], recv_sem=sem, device_id=to, device_id_type=MESH)
        index = count[0]
        count[0] += 1
        if guard is None:
            waits.append((c, when))
        else:
            later.append((index,) + guard)
        if when is None:
            c.start()
        else:
            pl.when(when)(c.start)

    def arrived(ref, sem):
        pltpu.make_async_copy(ref, ref, sem).wait()

    def vs(b, q):
        return v_ref.at[:, pl.ds(pl.multiple_of(b*SEGR + q*CH, 8), CH), :]

    def us(b, h):
        return u_ref.at[:, pl.ds(pl.multiple_of(b*128 + h*64, 64), 64), :]

    bar = pltpu.get_barrier_semaphore()

    def hello(to):
        pl.semaphore_signal(bar, inc=1, device_id=to, device_id_type=MESH)

    for c in range(2):
        for p in (1, 2, 3):
            hello(dev((x + p) % 4, y, z, c))
            hello(dev(x, (y + p) % 4, z, c))
            hello(dev(x, y, (z + p) % 4, c))
    hello(dev(x, y, z, 1 - k))
    for o in (pb, nb):
        hello((o % 8, o // 8))
    for xx in range(4):
        for yy in range(4):
            pl.when(jnp.logical_or(away, jnp.logical_or(x != xx, y != yy)))(lambda xx=xx, yy=yy: hello(dev(xx, yy, z, x_lo)))

    put_planes(su, unit(s_ref[...]))
    u_ref[:, 2080:2176, :] = jnp.zeros((2, 96, 128), F32)
    zero = jnp.zeros((1, 256), F32)
    put_planes(tails.at[0], jnp.concatenate([unit(st_ref[...]), zero], axis=0))
    put_planes(tails.at[1], jnp.concatenate([unit(at_ref[...]), zero], axis=0))
    pl.when(home)(lambda: pl.semaphore_wait(bar, 36))
    pl.when(away)(lambda: pl.semaphore_wait(bar, 37))

    for h in range(2):
        src = su.at[:, pl.ds(h*64, 64), :]
        own = pltpu.make_async_copy(src, us(col, h), got_u.at[col, h])
        pl.when(home)(own.start)
        remote(src, us(col, h), got_u.at[col, h], dev(x, y, z, 1 - k), away)
        for p in (1, 3):
            remote(src, us(col, h), got_u.at[col, h], dev((x + p*k) % 4, (y + p*(1 - k)) % 4, z, x_lo))
    up, dn, far = (z + 1) % 4, (z + 3) % 4, (z + 2) % 4
    bo = z*2 + k
    put_planes(v_ref.at[:, pl.ds(pl.multiple_of(bo*SEGR, 8), 512), :], unit(a_ref[...]))
    head = v_ref.at[:, pl.ds(pl.multiple_of(bo*SEGR, 8), 32), :]
    pz, pk = (pb % 8) // 2, (pb // 8) % 2
    remote(head, v_ref.at[:, pl.ds(pl.multiple_of((pz*2 + pk)*SEGR + 512, 8), 32), :], misc.at[1], (pb % 8, pb // 8), blk_no != 0)
    halo = v_ref.at[:, pl.ds(pl.multiple_of(bo*SEGR + 512, 8), 32), :]
    tv = pltpu.make_async_copy(tails.at[1], halo, misc.at[1])
    pl.when(blk_no == 127)(tv.start)

    def ring(q):
        for to in (dev(x, y, up, k), dev(x, y, dn, k), dev(x, y, z, 1 - k)):
            remote(vs(bo, q), vs(bo, q), got_v.at[bo, q], to)

    ring(0)
    ring(1)
    bu, bd, bf = up*2 + k, dn*2 + k, far*2 + k

    def near(q):
        for b, to, turn in ((bd, up, 0), (bu, dn, 1)):
            arrived(vs(b, q), got_v.at[b, q])
            if q % 2 == turn:
                remote(vs(b, q), vs(b, q), got_v.at[b, q], dev(x, y, to, k), guard=(0,))
            remote(vs(b, q), vs(b, q), got_v.at[b, q], dev(x, y, z, 1 - k), guard=(0,))

    def distant(q):
        arrived(vs(bf, q), got_v.at[bf, q])
        remote(vs(bf, q), vs(bf, q), got_v.at[bf, q], dev(x, y, z, 1 - k), guard=(0,))

    def others(q):
        for zz in range(4):
            b = zz*2 + 1 - k
            arrived(vs(b, q), got_v.at[b, q])

    def next_rows():
        pltpu.make_async_remote_copy(src_ref=u_ref.at[:, pl.ds(0, 32), :], dst_ref=u_ref.at[:, pl.ds(2048, 32), :], send_sem=misc.at[2], recv_sem=misc.at[0], device_id=dev(x, y, pr // 2, pr % 2), device_id_type=MESH).start()

    def stream(flag, cols, step):
        def blk(c, xc, d):
            return (cols[xc] // 2)*8 + ((y + d) % 4)*2 + c

        def get(c, xc, d):
            b = blk(c, xc, d)
            for h in range(2):
                arrived(us(b, h), got_u.at[b, h])
            if c == 0:
                pl.when(jnp.logical_and(b == 0, rb != 0))(next_rows)

        def put(c, xc, d, hs, *targets):
            b = blk(c, xc, d)
            for to in targets:
                for h in hs:
                    remote(us(b, h), us(b, h), got_u.at[b, h], to, guard=(0, flag))

        pl.when(flag)(lambda: step(get, put))

    def dx(p):
        return dev((x + p) % 4, y, z, k)

    def dy(p):
        return dev(x, (y + p) % 4, z, k)

    full = (0, 1)

    def h0(get, put):
        get(0, 0, 0)
        put(0, 0, 0, full, dx(1), dx(3))
        get(1, 0, 0)
        put(1, 0, 0, full, dy(1), dy(3))

    def h1(get, put):
        get(0, 0, 3)
        put(0, 0, 3, (0,), dy(1))
        put(0, 0, 3, full, dx(1), dx(3))
        get(0, 0, 1)
        put(0, 0, 1, (1,), dy(3))
        put(0, 0, 1, full, dx(1), dx(3))

    def h2(get, put):
        get(1, 1, 0)
        put(1, 1, 0, full, dy(1), dy(3))
        get(0, 0, 2)
        put(0, 0, 2, full, dx(1), dx(3))

    def yrelay(xc):
        def step(get, put):
            get(1, xc, 3)
            put(1, xc, 3, (0,), dy(1))
            get(1, xc, 1)
            put(1, xc, 1, (1,), dy(3))
        return step

    def h5(get, put):
        for xc in range(2):
            get(1, xc, 2)
        for d in range(4):
            get(0, 1, d)

    def away0(get, put):
        get(1, 0, 0)
        put(1, 0, 0, (0,), dx(1))
        put(1, 0, 0, full, dy(1), dy(3))
        get(1, 1, 0)
        put(1, 1, 0, (1,), dx(3))
        put(1, 1, 0, full, dy(1), dy(3))

    def away1(*ds):
        def step(get, put):
            for d in ds:
                get(0, 0, d)
                put(0, 0, d, (0,), dx(1))
                get(0, 1, d)
                put(0, 1, d, (1,), dx(3))
        return step

    def a5(get, put):
        for xc in range(2):
            get(1, xc, 2)

    hc = (x, (x + 2) % 4)
    ac = ((x + 3) % 4, (x + 1) % 4)

    def H(step):
        stream(home, hc, step)

    def A(step):
        stream(away, ac, step)

    H(h0)
    A(away0)
    near(0)
    ring(2)
    H(h1)
    A(away1(0))
    H(h2)
    A(yrelay(0))
    A(yrelay(1))
    near(1)
    tv.wait()
    ring(3)
    H(yrelay(0))
    A(away1(3))
    A(away1(1))
    H(yrelay(1))
    A(away1(2))
    H(h5)
    A(a5)
    tu = pltpu.make_async_copy(tails.at[0], u_ref.at[:, pl.ds(2048, 32), :], misc.at[0])
    pl.when(rb == 7)(tu.start)
    distant(0)
    distant(1)
    tu.wait()
    prep_rhs(u_ref, bt)
    others(0)
    near(2)
    others(1)

    def service(m):
        def first():
            near(3)
            distant(2)

        def third():
            distant(3)

        pl.when(m == 0)(first)
        pl.when(m == 1)(lambda: others(2))
        pl.when(m == 2)(third)
        pl.when(m == 3)(lambda: others(3))

    acc[...] = jnp.full(acc.shape, NEG, F32)
    R = compute(v_ref, [a0, a1, a2], bt, [g0, g1, g2], acc, service)
    finish(acc, R, colm, rowm)
    for c, when in waits:
        if when is None:
            c.wait_send()
        else:
            pl.when(when)(c.wait_send)
    pl.when(rb != 0)(lambda: arrived(u_ref.at[:, pl.ds(0, 32), :], misc.at[2]))
    for index, *how in later:
        if len(how) == 1:
            arrived(vs(0, 0), send.at[index])
        else:
            pl.when(how[1])(lambda index=index: arrived(us(0, 0), send.at[index]))
    cp = []
    for s in range(8):
        other = rb != s
        c = pltpu.make_async_remote_copy(src_ref=colm.at[s], dst_ref=cbuf.at[rb], send_sem=csend.at[s], recv_sem=cgot.at[rb], device_id=dev(x, y, s // 2, s % 2), device_id_type=MESH)
        pl.when(other)(c.start)
        cp.append((c, other))
    for j in range(16):
        other = jnp.logical_or(col != j, away)
        c = pltpu.make_async_remote_copy(src_ref=rowm.at[j], dst_ref=rbuf.at[me_r], send_sem=rsend.at[j], recv_sem=rgot.at[me_r], device_id=(rb, j), device_id_type=MESH)
        pl.when(other)(c.start)
        cp.append((c, other))
    lc = pltpu.make_async_copy(colm.at[rb], cbuf.at[rb], cgot.at[rb])
    lr = pltpu.make_async_copy(rowm.at[col], rbuf.at[me_r], rgot.at[me_r])
    lc.start()
    pl.when(home)(lr.start)
    for s in range(8):
        arrived(cbuf.at[s], cgot.at[s])
    for j in range(16):
        arrived(rbuf.at[j], rgot.at[j])
    colp_ref[...] = functools.reduce(jnp.maximum, [cbuf[s] for s in range(8)])
    rowp_ref[...] = functools.reduce(jnp.maximum, [rbuf[j] for j in range(16)])
    for c, other in cp:
        pl.when(other)(c.wait_send)

def on_device(stream, stream_tail, archive, archive_tail):
    DMA = pltpu.SemaphoreType.DMA
    col, row = pl.pallas_call(
        kern,
        out_shape=(jax.ShapeDtypeStruct((1, 512), F32), jax.ShapeDtypeStruct((1, 128), F32)),
        in_specs=[VM]*4, out_specs=(VM, VM),
        scratch_shapes=[
            pltpu.VMEM((2, 8*SEGR, 128), F32), pltpu.VMEM((2, 2176, 128), F32),
            pltpu.VMEM((2, 128, 128), F32), pltpu.VMEM((2, 2, 32, 128), F32),
            pltpu.VMEM((256, 768), jnp.bfloat16), pltpu.VMEM((256, 768), jnp.bfloat16), pltpu.VMEM((256, 768), jnp.bfloat16), pltpu.VMEM((C*BR, 768), jnp.bfloat16),
            pltpu.VMEM((256, C*128), F32), pltpu.VMEM((256, C*128), F32), pltpu.VMEM((256, C*128), F32),
            pltpu.VMEM((8, 640), F32),
            pltpu.VMEM((8, 1, 512), F32), pltpu.VMEM((16, 1, 128), F32),
            pltpu.VMEM((8, 1, 512), F32), pltpu.VMEM((16, 1, 128), F32),
            DMA((140,)), DMA((8, NQ)), DMA((16, 2)), DMA((3,)),
            DMA((8,)), DMA((16,)), DMA((8,)), DMA((16,)),
        ],
        compiler_params=pltpu.CompilerParams(has_side_effects=True, collective_id=0, vmem_limit_bytes=67043328),
        name="join_profile")(stream, stream_tail, archive, archive_tail)
    return row.reshape(-1), col.reshape(-1)

def solution(mesh):
    return jax.shard_map(
        on_device, mesh=mesh,
        in_specs=(P(("row", "col"), None), P(), P(("col", "row"), None), P()),
        out_specs=(P(("row", "col")), P(("col", "row"))),
        check_vma=False)
```

```python
import functools

import jax
import jax.numpy as jnp
from jax import lax
from jax.sharding import PartitionSpec as P
from jax.experimental import pallas as pl
from jax.experimental.pallas import tpu as pltpu

M=32; C=17; SEGR=544; T=544; TV=512; NB=17; BR=384
NEG=-64.0
DN = (((1,), (0,)), ((), ()))
DT = (((1,), (1,)), ((), ()))
S = 32.0
def split_left(x):
    hi = x.astype(jnp.bfloat16)
    top = hi.astype(jnp.float32)
    return hi, (top + S*(x - top)).astype(jnp.bfloat16)
def split_right(y):
    most = y*(1.0 - 1.0/S)
    hi = most.astype(jnp.bfloat16)
    return hi, (y*(1.0/S) + (most - hi.astype(jnp.float32))).astype(jnp.bfloat16)
def prep_rhs(u_ref, b_ref):
    def one(c, _):
        for a in range(8):
            x = [[u_ref.at[p][pl.ds(c + 34*a + 17*h, 8, stride=272), :] for p in range(2)] for h in range(2)]
            for w in range(3):
                y = jnp.concatenate([jnp.concatenate(x[h], axis=1) for h in range(2)], axis=0)
                hi, lo = split_right(y)
                r = pl.multiple_of(c*BR + 16*(a + 8*w), 16)
                b_ref[pl.ds(r, 16), 0:256] = hi
                b_ref[pl.ds(r, 16), 256:512] = lo
                if w < 2:
                    x = [[pltpu.roll(t, 7, 0) for t in row] for row in x]
        return 0
    lax.fori_loop(0, C, one, 0)
def prep_lhs(v_ref, a_ref, n, part=range(16)):
    for i in part:
        x = jnp.concatenate([jnp.concatenate([v_ref.at[p][pl.ds(n*32 + 2*i + d, 8, stride=SEGR), :] for p in range(2)], axis=1) for d in range(2)], axis=0)
        hi, lo = split_left(x)
        a_ref[16*i:16*i+16, 0:256] = hi
        a_ref[16*i:16*i+16, 256:512] = lo
def mm(a_ref, b_ref, g_ref, n, tiles=range(9)):
    def rows(c):
        return b_ref[pl.ds(pl.multiple_of(c*BR + n*16, 16), 128), :]
    for j in tiles:
        cs = [2*j, 2*j+1] if j < 8 else [16]
        b = jnp.concatenate([rows(c) for c in cs], axis=0)
        g_ref[:, cs[0]*128:(cs[-1]+1)*128] = lax.dot_general(a_ref[...], b, DT, preferred_element_type=jnp.float32)
def seg_of(lane, n):
    return (2*n + 2*(lane >> 4) + ((lane >> 3) & 1) + 16*(lane & 7)) & 127
def lane_of(seg):
    s = seg & 127
    return ((s & 15) >> 1)*16 + (s & 1)*8 + (s >> 4)
def take(x, idx):
    return jnp.take_along_axis(x, idx, axis=1)
def vblock(cur, prev, n, E, R, acc_ref, lo, hi, beside=None):
    lane = lax.broadcasted_iota(jnp.int32, (8,128), 1)
    rel = seg_of(lane, 0)
    prv1, nxt1, nxt2 = lane_of(rel + 127), lane_of(rel + 1), lane_of(rel + 2)
    sg = seg_of(lane, n)
    keepx = (sg >= 2) & (sg <= 121)
    keepb = (sg >= 2) & (sg <= 122)
    keepc = (sg >= 1) & (sg <= 121)
    neg = jnp.float32(NEG)
    E = [take(e, nxt2) for e in E]
    R = [take(r, nxt2) for r in R]
    for k in range(32):
        if beside is not None and k % 4 == 0:
            beside(k // 4)
        g = lambda ref, c: ref[k*8:k*8+8, c*128:(c+1)*128]
        N = []
        for c in range(C):
            old = g(prev, c+2) if c < 15 else take(g(prev, c-15), nxt1)
            ep = E[c-1] if c else take(E[C-1], prv1)
            N.append(ep + (g(cur, c) - old))
        E = N
        if lo <= k < hi:
            R = [jnp.maximum(r, e) for r, e in zip(R, E)]
            mx = functools.reduce(jnp.maximum, E[5:14])
            mb = functools.reduce(jnp.maximum, E[0:5])
            mc = functools.reduce(jnp.maximum, E[14:17])
            m = jnp.maximum(jnp.where(keepx, mx, neg), jnp.maximum(jnp.where(keepb, mb, neg), jnp.where(keepc, mc, neg)))
            acc_ref[pl.ds(pl.multiple_of((n*32 + k - 31)*8, 8), 8), :] = m
    if beside is not None:
        beside(8)
    return E, R
def compute(v_ref, a, b_ref, gs, acc_ref, service):
    z = jnp.zeros((8,128), jnp.float32)
    E = [z]*C
    R = [jnp.full((8,128), NEG, jnp.float32)]*C
    gs[2][...] = jnp.zeros(gs[2].shape, jnp.float32)
    first = jnp.int32(0)
    for n in range(3):
        prep_lhs(v_ref, a[n], n)
    mm(a[0], b_ref, gs[0], 0)
    E, R = vblock(gs[0], gs[2], first, E, R, acc_ref, 31, 32, lambda j: mm(a[1], b_ref, gs[1], 1, [j]))
    def three(m, carry):
        E, R = list(carry[0]), list(carry[1])
        service(m)
        for r in range(3):
            n = 1 + 3*m + r
            def beside(j, n=n, r=r):
                mm(a[(2+r)%3], b_ref, gs[(2+r)%3], n+1, [j])
                if j < 8:
                    prep_lhs(v_ref, a[r%3], jnp.minimum(n+2, NB-1), [2*j, 2*j+1])
            E, R = vblock(gs[(1+r)%3], gs[r%3], n, E, R, acc_ref, 0, 32, beside)
        return tuple(E), tuple(R)
    E, R = lax.fori_loop(0, 5, three, (tuple(E), tuple(R)))
    E, R = vblock(gs[1], gs[0], first + 16, list(E), list(R), acc_ref, 0, 31)
    lane = lax.broadcasted_iota(jnp.int32, (8,128), 1)
    back = lane_of(lane - 32)
    return [take(r, back) for r in R]
def finish(acc_ref, R, col_ref, row_ref):
    def one(s, _):
        for tb in range(4):
            x = acc_ref[pl.ds(s + tb*1024, 128, stride=8), :]
            col_ref[s, 0:1, tb*128:(tb+1)*128] = jnp.max(x.T, axis=0, keepdims=True)*(1.0/M)
        return 0
    lax.fori_loop(0, 8, one, 0)
    rows = jnp.concatenate([jnp.max(r, axis=0, keepdims=True) for r in R] + [jnp.full((7, 128), NEG, jnp.float32)], axis=0)*(1.0/M)
    for j in range(4):
        q = lax.broadcasted_iota(jnp.int32, (128, 512), 1) + (31 + 512*j)
        pick = (lax.broadcasted_iota(jnp.int32, (128, 512), 0) == ((q*3856) >> 16)).astype(jnp.float32)
        x = lax.dot_general(rows, pick, DN, precision=lax.Precision.HIGHEST, preferred_element_type=jnp.float32)
        q = lax.broadcasted_iota(jnp.int32, (24, 512), 1) + (31 + 512*j)
        lane = (q*3856) >> 16
        x = jnp.where(lax.broadcasted_iota(jnp.int32, (24, 512), 0) == q - lane*C, x, 0.0)
        x = jnp.sum(x, axis=0, keepdims=True)
        for m in range(4):
            row_ref[4*j + m, 0:1, :] = x[:, 128*m:128*(m+1)]
VM = pl.BlockSpec(memory_space=pltpu.VMEM)
F32 = jnp.float32
MESH = pl.DeviceIdType.MESH
NQ = 4
CH = SEGR // NQ

def dev(x, y, z, k):
    return (z*2 + x % 2, (x // 2)*8 + y*2 + k)

def unit(x):
    return x * (1.0 / jnp.sqrt(jnp.sum(x*x, axis=1, keepdims=True) + 1e-06))

def put_planes(dst, x):
    dst[0] = x[:, :128]
    dst[1] = x[:, 128:]

def kern(s_ref, st_ref, a_ref, at_ref, colp_ref, rowp_ref, v_ref, u_ref, su, tails, a0, a1, a2, bt, g0, g1, g2, acc,
         colm, rowm, cbuf, rbuf, send, got_v, got_u, misc, csend, rsend, cgot, rgot):
    row, col = lax.axis_index("row"), lax.axis_index("col")
    z, x_lo = row // 2, row % 2
    x_hi, y, k = col // 8, (col // 2) % 4, col % 2
    x = x_hi*2 + x_lo
    home = x_lo == k
    away = x_lo != k
    rb = z*2 + k
    me_r = x_hi*8 + y*2 + x_lo
    blk_no = col*8 + row
    pb, nb = (blk_no + 127) % 128, (blk_no + 1) % 128
    pr = (rb + 7) % 8
    waits, later = [], []
    count = [0]

    def remote(src, dst, sem, to, when=None, guard=None):
        c = pltpu.make_async_remote_copy(src_ref=src, dst_ref=dst, send_sem=send.at[count[0]], recv_sem=sem, device_id=to, device_id_type=MESH)
        index = count[0]
        count[0] += 1
        if guard is None:
            waits.append((c, when))
        else:
            later.append((index,) + guard)
        if when is None:
            c.start()
        else:
            pl.when(when)(c.start)

    def arrived(ref, sem):
        pltpu.make_async_copy(ref, ref, sem).wait()

    def vs(b, q):
        return v_ref.at[:, pl.ds(pl.multiple_of(b*SEGR + q*CH, 8), CH), :]

    def us(b, h):
        return u_ref.at[:, pl.ds(pl.multiple_of(b*128 + h*64, 64), 64), :]

    bar = pltpu.get_barrier_semaphore()

    def hello(to):
        pl.semaphore_signal(bar, inc=1, device_id=to, device_id_type=MESH)

    for c in range(2):
        for p in (1, 2, 3):
            hello(dev((x + p) % 4, y, z, c))
            hello(dev(x, (y + p) % 4, z, c))
            hello(dev(x, y, (z + p) % 4, c))
    hello(dev(x, y, z, 1 - k))
    for o in (pb, nb):
        hello((o % 8, o // 8))
    for xx in range(4):
        for yy in range(4):
            pl.when(jnp.logical_or(away, jnp.logical_or(x != xx, y != yy)))(lambda xx=xx, yy=yy: hello(dev(xx, yy, z, x_lo)))

    put_planes(su, unit(s_ref[...]))
    u_ref[:, 2080:2176, :] = jnp.zeros((2, 96, 128), F32)
    zero = jnp.zeros((1, 256), F32)
    put_planes(tails.at[0], jnp.concatenate([unit(st_ref[...]), zero], axis=0))
    put_planes(tails.at[1], jnp.concatenate([unit(at_ref[...]), zero], axis=0))
    pl.when(home)(lambda: pl.semaphore_wait(bar, 36))
    pl.when(away)(lambda: pl.semaphore_wait(bar, 37))

    for h in range(2):
        src = su.at[:, pl.ds(h*64, 64), :]
        own = pltpu.make_async_copy(src, us(col, h), got_u.at[col, h])
        pl.when(home)(own.start)
        remote(src, us(col, h), got_u.at[col, h], dev(x, y, z, 1 - k), away)
        for p in (1, 3):
            remote(src, us(col, h), got_u.at[col, h], dev((x + p*k) % 4, (y + p*(1 - k)) % 4, z, x_lo))
    up, dn, far = (z + 1) % 4, (z + 3) % 4, (z + 2) % 4
    bo = z*2 + k
    put_planes(v_ref.at[:, pl.ds(pl.multiple_of(bo*SEGR, 8), 512), :], unit(a_ref[...]))
    head = v_ref.at[:, pl.ds(pl.multiple_of(bo*SEGR, 8), 32), :]
    pz, pk = (pb % 8) // 2, (pb // 8) % 2
    remote(head, v_ref.at[:, pl.ds(pl.multiple_of((pz*2 + pk)*SEGR + 512, 8), 32), :], misc.at[1], (pb % 8, pb // 8), blk_no != 0)
    halo = v_ref.at[:, pl.ds(pl.multiple_of(bo*SEGR + 512, 8), 32), :]
    tv = pltpu.make_async_copy(tails.at[1], halo, misc.at[1])
    pl.when(blk_no == 127)(tv.start)

    def ring(q):
        for to in (dev(x, y, up, k), dev(x, y, dn, k), dev(x, y, z, 1 - k)):
            remote(vs(bo, q), vs(bo, q), got_v.at[bo, q], to)

    ring(0)
    ring(1)
    bu, bd, bf = up*2 + k, dn*2 + k, far*2 + k

    def near(q):
        for b, to, turn in ((bd, up, 0), (bu, dn, 1)):
            arrived(vs(b, q), got_v.at[b, q])
            if q % 2 == turn:
                remote(vs(b, q), vs(b, q), got_v.at[b, q], dev(x, y, to, k), guard=(0,))
            remote(vs(b, q), vs(b, q), got_v.at[b, q], dev(x, y, z, 1 - k), guard=(0,))

    def distant(q):
        arrived(vs(bf, q), got_v.at[bf, q])
        remote(vs(bf, q), vs(bf, q), got_v.at[bf, q], dev(x, y, z, 1 - k), guard=(0,))

    def others(q):
        for zz in range(4):
            b = zz*2 + 1 - k
            arrived(vs(b, q), got_v.at[b, q])

    def next_rows():
        pltpu.make_async_remote_copy(src_ref=u_ref.at[:, pl.ds(0, 32), :], dst_ref=u_ref.at[:, pl.ds(2048, 32), :], send_sem=misc.at[2], recv_sem=misc.at[0], device_id=dev(x, y, pr // 2, pr % 2), device_id_type=MESH).start()

    def stream(flag, cols, step):
        def blk(c, xc, d):
            return (cols[xc] // 2)*8 + ((y + d) % 4)*2 + c

        def get(c, xc, d):
            b = blk(c, xc, d)
            for h in range(2):
                arrived(us(b, h), got_u.at[b, h])
            if c == 0:
                pl.when(jnp.logical_and(b == 0, rb != 0))(next_rows)

        def put(c, xc, d, hs, *targets):
            b = blk(c, xc, d)
            for to in targets:
                for h in hs:
                    remote(us(b, h), us(b, h), got_u.at[b, h], to, guard=(0, flag))

        pl.when(flag)(lambda: step(get, put))

    def dx(p):
        return dev((x + p) % 4, y, z, k)

    def dy(p):
        return dev(x, (y + p) % 4, z, k)

    full = (0, 1)

    def h0(get, put):
        get(0, 0, 0)
        put(0, 0, 0, full, dx(1), dx(3))
        get(1, 0, 0)
        put(1, 0, 0, full, dy(1), dy(3))

    def h1(get, put):
        get(0, 0, 3)
        put(0, 0, 3, (0,), dy(1))
        put(0, 0, 3, full, dx(1), dx(3))
        get(0, 0, 1)
        put(0, 0, 1, (1,), dy(3))
        put(0, 0, 1, full, dx(1), dx(3))

    def h2(get, put):
        get(1, 1, 0)
        put(1, 1, 0, full, dy(1), dy(3))
        get(0, 0, 2)
        put(0, 0, 2, full, dx(1), dx(3))

    def yrelay(xc):
        def step(get, put):
            get(1, xc, 3)
            put(1, xc, 3, (0,), dy(1))
            get(1, xc, 1)
            put(1, xc, 1, (1,), dy(3))
        return step

    def h5(get, put):
        for xc in range(2):
            get(1, xc, 2)
        for d in range(4):
            get(0, 1, d)

    def away0(get, put):
        get(1, 0, 0)
        put(1, 0, 0, (0,), dx(1))
        put(1, 0, 0, full, dy(1), dy(3))
        get(1, 1, 0)
        put(1, 1, 0, (1,), dx(3))
        put(1, 1, 0, full, dy(1), dy(3))

    def away1(*ds):
        def step(get, put):
            for d in ds:
                get(0, 0, d)
                put(0, 0, d, (0,), dx(1))
                get(0, 1, d)
                put(0, 1, d, (1,), dx(3))
        return step

    def a5(get, put):
        for xc in range(2):
            get(1, xc, 2)

    hc = (x, (x + 2) % 4)
    ac = ((x + 3) % 4, (x + 1) % 4)

    def H(step):
        stream(home, hc, step)

    def A(step):
        stream(away, ac, step)

    H(h0)
    A(away0)
    near(0)
    ring(2)
    H(h1)
    A(away1(0))
    H(h2)
    A(yrelay(0))
    A(yrelay(1))
    near(1)
    tv.wait()
    ring(3)
    H(yrelay(0))
    A(away1(3))
    A(away1(1))
    H(yrelay(1))
    A(away1(2))
    H(h5)
    A(a5)
    tu = pltpu.make_async_copy(tails.at[0], u_ref.at[:, pl.ds(2048, 32), :], misc.at[0])
    pl.when(rb == 7)(tu.start)
    distant(0)
    distant(1)
    tu.wait()
    prep_rhs(u_ref, bt)
    others(0)
    near(2)
    others(1)

    def service(m):
        def first():
            near(3)
            distant(2)

        def third():
            distant(3)

        pl.when(m == 0)(first)
        pl.when(m == 1)(lambda: others(2))
        pl.when(m == 2)(third)
        pl.when(m == 3)(lambda: others(3))

    R = compute(v_ref, [a0, a1, a2], bt, [g0, g1, g2], acc, service)
    finish(acc, R, colm, rowm)
    for c, when in waits:
        if when is None:
            c.wait_send()
        else:
            pl.when(when)(c.wait_send)
    pl.when(rb != 0)(lambda: arrived(u_ref.at[:, pl.ds(0, 32), :], misc.at[2]))
    for index, *how in later:
        if len(how) == 1:
            arrived(vs(0, 0), send.at[index])
        else:
            pl.when(how[1])(lambda index=index: arrived(us(0, 0), send.at[index]))
    cp = []
    for s in range(8):
        other = rb != s
        c = pltpu.make_async_remote_copy(src_ref=colm.at[s], dst_ref=cbuf.at[rb], send_sem=csend.at[s], recv_sem=cgot.at[rb], device_id=dev(x, y, s // 2, s % 2), device_id_type=MESH)
        pl.when(other)(c.start)
        cp.append((c, other))
    for j in range(16):
        other = jnp.logical_or(col != j, away)
        c = pltpu.make_async_remote_copy(src_ref=rowm.at[j], dst_ref=rbuf.at[me_r], send_sem=rsend.at[j], recv_sem=rgot.at[me_r], device_id=(rb, j), device_id_type=MESH)
        pl.when(other)(c.start)
        cp.append((c, other))
    lc = pltpu.make_async_copy(colm.at[rb], cbuf.at[rb], cgot.at[rb])
    lr = pltpu.make_async_copy(rowm.at[col], rbuf.at[me_r], rgot.at[me_r])
    lc.start()
    pl.when(home)(lr.start)
    for s in range(8):
        arrived(cbuf.at[s], cgot.at[s])
    for j in range(16):
        arrived(rbuf.at[j], rgot.at[j])
    colp_ref[...] = functools.reduce(jnp.maximum, [cbuf[s] for s in range(8)])
    rowp_ref[...] = functools.reduce(jnp.maximum, [rbuf[j] for j in range(16)])
    for c, other in cp:
        pl.when(other)(c.wait_send)

def on_device(stream, stream_tail, archive, archive_tail):
    DMA = pltpu.SemaphoreType.DMA
    col, row = pl.pallas_call(
        kern,
        out_shape=(jax.ShapeDtypeStruct((1, 512), F32), jax.ShapeDtypeStruct((1, 128), F32)),
        in_specs=[VM]*4, out_specs=(VM, VM),
        scratch_shapes=[
            pltpu.VMEM((2, 8*SEGR, 128), F32), pltpu.VMEM((2, 2176, 128), F32),
            pltpu.VMEM((2, 128, 128), F32), pltpu.VMEM((2, 2, 32, 128), F32),
            pltpu.VMEM((256, 512), jnp.bfloat16), pltpu.VMEM((256, 512), jnp.bfloat16), pltpu.VMEM((256, 512), jnp.bfloat16), pltpu.VMEM((C*BR, 512), jnp.bfloat16),
            pltpu.VMEM((256, C*128), F32), pltpu.VMEM((256, C*128), F32), pltpu.VMEM((256, C*128), F32),
            pltpu.VMEM((4096, 128), F32),
            pltpu.VMEM((8, 1, 512), F32), pltpu.VMEM((16, 1, 128), F32),
            pltpu.VMEM((8, 1, 512), F32), pltpu.VMEM((16, 1, 128), F32),
            DMA((140,)), DMA((8, NQ)), DMA((16, 2)), DMA((3,)),
            DMA((8,)), DMA((16,)), DMA((8,)), DMA((16,)),
        ],
        compiler_params=pltpu.CompilerParams(has_side_effects=True, collective_id=0, vmem_limit_bytes=67043328),
        name="join_profile")(stream, stream_tail, archive, archive_tail)
    return row.reshape(-1), col.reshape(-1)

def solution(mesh):
    return jax.shard_map(
        on_device, mesh=mesh,
        in_specs=(P(("row", "col"), None), P(), P(("col", "row"), None), P()),
        out_specs=(P(("row", "col")), P(("col", "row"))),
        check_vma=False)
```

```python
import functools

import jax
import jax.numpy as jnp
from jax import lax
from jax.sharding import PartitionSpec as P
from jax.experimental import pallas as pl
from jax.experimental.pallas import tpu as pltpu

M=32; C=17; SEGR=544; T=544; TV=512; NB=17; BR=384
NEG=-64.0
DN = (((1,), (0,)), ((), ()))
DT = (((1,), (1,)), ((), ()))
S = 32.0
def split_left(x):
    hi = x.astype(jnp.bfloat16)
    top = hi.astype(jnp.float32)
    return hi, (top + S*(x - top)).astype(jnp.bfloat16)
def split_right(y):
    most = y*(1.0 - 1.0/S)
    hi = most.astype(jnp.bfloat16)
    return hi, (y*(1.0/S) + (most - hi.astype(jnp.float32))).astype(jnp.bfloat16)
def prep_rhs(u_ref, b_ref):
    def one(c, _):
        for a in range(8):
            x = [[u_ref.at[p][pl.ds(c + 34*a + 17*h, 8, stride=272), :] for p in range(2)] for h in range(2)]
            for w in range(3):
                y = jnp.concatenate([jnp.concatenate(x[h], axis=1) for h in range(2)], axis=0)
                hi, lo = split_right(y)
                r = pl.multiple_of(c*BR + 16*(a + 8*w), 16)
                b_ref[pl.ds(r, 16), 0:256] = hi
                b_ref[pl.ds(r, 16), 256:512] = lo
                if w < 2:
                    x = [[pltpu.roll(t, 7, 0) for t in row] for row in x]
        return 0
    lax.fori_loop(0, C, one, 0)
def prep_lhs(v_ref, a_ref, n, part=range(16)):
    for i in part:
        x = jnp.concatenate([jnp.concatenate([v_ref.at[p][pl.ds(n*32 + 2*i + d, 8, stride=SEGR), :] for p in range(2)], axis=1) for d in range(2)], axis=0)
        hi, lo = split_left(x)
        a_ref[16*i:16*i+16, 0:256] = hi
        a_ref[16*i:16*i+16, 256:512] = lo
def mm(a_ref, b_ref, g_ref, n, tiles=range(9)):
    def rows(c):
        return b_ref[pl.ds(pl.multiple_of(c*BR + n*16, 16), 128), :]
    for j in tiles:
        cs = [2*j, 2*j+1] if j < 8 else [16]
        b = jnp.concatenate([rows(c) for c in cs], axis=0)
        g_ref[:, cs[0]*128:(cs[-1]+1)*128] = lax.dot_general(a_ref[...], b, DT, preferred_element_type=jnp.float32)
def seg_of(lane, n):
    return (2*n + 2*(lane >> 4) + ((lane >> 3) & 1) + 16*(lane & 7)) & 127
def lane_of(seg):
    s = seg & 127
    return ((s & 15) >> 1)*16 + (s & 1)*8 + (s >> 4)
def take(x, idx):
    return jnp.take_along_axis(x, idx, axis=1)
def vblock(cur, prev, n, E, R, acc_ref, lo, hi, beside=None):
    lane = lax.broadcasted_iota(jnp.int32, (8,128), 1)
    rel = seg_of(lane, 0)
    prv1, nxt1, nxt2 = lane_of(rel + 127), lane_of(rel + 1), lane_of(rel + 2)
    sg = seg_of(lane, n)
    keepx = (sg >= 2) & (sg <= 121)
    keepb = (sg >= 2) & (sg <= 122)
    keepc = (sg >= 1) & (sg <= 121)
    neg = jnp.float32(NEG)
    E = [take(e, nxt2) for e in E]
    R = [take(r, nxt2) for r in R]
    for k in range(32):
        if beside is not None and k % 4 == 0:
            beside(k // 4)
        g = lambda ref, c: ref[k*8:k*8+8, c*128:(c+1)*128]
        N = []
        for c in range(C):
            old = g(prev, c+2) if c < 15 else take(g(prev, c-15), nxt1)
            ep = E[c-1] if c else take(E[C-1], prv1)
            N.append(ep + (g(cur, c) - old))
        E = N
        if lo <= k < hi:
            R = [jnp.maximum(r, e) for r, e in zip(R, E)]
            mx = functools.reduce(jnp.maximum, E[5:14])
            mb = functools.reduce(jnp.maximum, E[0:5])
            mc = functools.reduce(jnp.maximum, E[14:17])
            m = jnp.maximum(jnp.where(keepx, mx, neg), jnp.maximum(jnp.where(keepb, mb, neg), jnp.where(keepc, mc, neg)))
            acc_ref[pl.ds(pl.multiple_of((n*32 + k - 31)*8, 8), 8), :] = m
    if beside is not None:
        beside(8)
    return E, R
def compute(v_ref, a, b_ref, gs, acc_ref, service):
    z = jnp.zeros((8,128), jnp.float32)
    E = [z]*C
    R = [jnp.full((8,128), NEG, jnp.float32)]*C
    gs[2][...] = jnp.zeros(gs[2].shape, jnp.float32)
    first = jnp.int32(0)
    for n in range(3):
        prep_lhs(v_ref, a[n], n)
    mm(a[0], b_ref, gs[0], 0)
    E, R = vblock(gs[0], gs[2], first, E, R, acc_ref, 31, 32, lambda j: mm(a[1], b_ref, gs[1], 1, [j]))
    def three(m, carry):
        E, R = list(carry[0]), list(carry[1])
        service(m)
        for r in range(3):
            n = 1 + 3*m + r
            def beside(j, n=n, r=r):
                mm(a[(2+r)%3], b_ref, gs[(2+r)%3], n+1, [j])
                if j < 8:
                    prep_lhs(v_ref, a[r%3], jnp.minimum(n+2, NB-1), [2*j, 2*j+1])
            E, R = vblock(gs[(1+r)%3], gs[r%3], n, E, R, acc_ref, 0, 32, beside)
        return tuple(E), tuple(R)
    E, R = lax.fori_loop(0, 5, three, (tuple(E), tuple(R)))
    E, R = vblock(gs[1], gs[0], first + 16, list(E), list(R), acc_ref, 0, 31)
    lane = lax.broadcasted_iota(jnp.int32, (8,128), 1)
    back = lane_of(lane - 32)
    return [take(r, back) for r in R]
def finish_cols(acc_ref, col_ref):
    def one(s, _):
        for tb in range(4):
            x = acc_ref[pl.ds(s + tb*1024, 128, stride=8), :]
            col_ref[s, 0:1, tb*128:(tb+1)*128] = jnp.max(x.T, axis=0, keepdims=True)*(1.0/M)
        return 0
    lax.fori_loop(0, 8, one, 0)
def finish_rows(R, row_ref):
    rows = jnp.concatenate([jnp.max(r, axis=0, keepdims=True) for r in R] + [jnp.full((7, 128), NEG, jnp.float32)], axis=0)*(1.0/M)
    for j in range(4):
        q = lax.broadcasted_iota(jnp.int32, (128, 512), 1) + (31 + 512*j)
        pick = (lax.broadcasted_iota(jnp.int32, (128, 512), 0) == ((q*3856) >> 16)).astype(jnp.float32)
        x = lax.dot_general(rows, pick, DN, precision=lax.Precision.HIGHEST, preferred_element_type=jnp.float32)
        q = lax.broadcasted_iota(jnp.int32, (24, 512), 1) + (31 + 512*j)
        lane = (q*3856) >> 16
        x = jnp.where(lax.broadcasted_iota(jnp.int32, (24, 512), 0) == q - lane*C, x, 0.0)
        x = jnp.sum(x, axis=0, keepdims=True)
        for m in range(4):
            row_ref[4*j + m, 0:1, :] = x[:, 128*m:128*(m+1)]
VM = pl.BlockSpec(memory_space=pltpu.VMEM)
F32 = jnp.float32
MESH = pl.DeviceIdType.MESH
NQ = 4
CH = SEGR // NQ

def dev(x, y, z, k):
    return (z*2 + x % 2, (x // 2)*8 + y*2 + k)

def unit(x):
    return x * (1.0 / jnp.sqrt(jnp.sum(x*x, axis=1, keepdims=True) + 1e-06))

def put_planes(dst, x):
    dst[0] = x[:, :128]
    dst[1] = x[:, 128:]

def kern(s_ref, st_ref, a_ref, at_ref, colp_ref, rowp_ref, v_ref, u_ref, su, tails, a0, a1, a2, bt, g0, g1, g2, acc,
         colm, rowm, cbuf, rbuf, send, got_v, got_u, misc, csend, rsend, cgot, rgot):
    row, col = lax.axis_index("row"), lax.axis_index("col")
    z, x_lo = row // 2, row % 2
    x_hi, y, k = col // 8, (col // 2) % 4, col % 2
    x = x_hi*2 + x_lo
    home = x_lo == k
    away = x_lo != k
    rb = z*2 + k
    me_r = x_hi*8 + y*2 + x_lo
    blk_no = col*8 + row
    pb, nb = (blk_no + 127) % 128, (blk_no + 1) % 128
    pr = (rb + 7) % 8
    waits, later = [], []
    count = [0]

    def remote(src, dst, sem, to, when=None, guard=None):
        c = pltpu.make_async_remote_copy(src_ref=src, dst_ref=dst, send_sem=send.at[count[0]], recv_sem=sem, device_id=to, device_id_type=MESH)
        index = count[0]
        count[0] += 1
        if guard is None:
            waits.append((c, when))
        else:
            later.append((index,) + guard)
        if when is None:
            c.start()
        else:
            pl.when(when)(c.start)

    def arrived(ref, sem):
        pltpu.make_async_copy(ref, ref, sem).wait()

    def vs(b, q):
        return v_ref.at[:, pl.ds(pl.multiple_of(b*SEGR + q*CH, 8), CH), :]

    def us(b, h):
        return u_ref.at[:, pl.ds(pl.multiple_of(b*128 + h*64, 64), 64), :]

    bar = pltpu.get_barrier_semaphore()

    def hello(to):
        pl.semaphore_signal(bar, inc=1, device_id=to, device_id_type=MESH)

    for c in range(2):
        for p in (1, 2, 3):
            hello(dev((x + p) % 4, y, z, c))
            hello(dev(x, (y + p) % 4, z, c))
            hello(dev(x, y, (z + p) % 4, c))
    hello(dev(x, y, z, 1 - k))
    for o in (pb, nb):
        hello((o % 8, o // 8))
    for xx in range(4):
        for yy in range(4):
            pl.when(jnp.logical_or(away, jnp.logical_or(x != xx, y != yy)))(lambda xx=xx, yy=yy: hello(dev(xx, yy, z, x_lo)))

    put_planes(su, unit(s_ref[...]))
    u_ref[:, 2080:2176, :] = jnp.zeros((2, 96, 128), F32)
    zero = jnp.zeros((1, 256), F32)
    put_planes(tails.at[0], jnp.concatenate([unit(st_ref[...]), zero], axis=0))
    put_planes(tails.at[1], jnp.concatenate([unit(at_ref[...]), zero], axis=0))
    pl.when(home)(lambda: pl.semaphore_wait(bar, 36))
    pl.when(away)(lambda: pl.semaphore_wait(bar, 37))

    for h in range(2):
        src = su.at[:, pl.ds(h*64, 64), :]
        own = pltpu.make_async_copy(src, us(col, h), got_u.at[col, h])
        pl.when(home)(own.start)
        remote(src, us(col, h), got_u.at[col, h], dev(x, y, z, 1 - k), away)
        for p in (1, 3):
            remote(src, us(col, h), got_u.at[col, h], dev((x + p*k) % 4, (y + p*(1 - k)) % 4, z, x_lo))
    up, dn, far = (z + 1) % 4, (z + 3) % 4, (z + 2) % 4
    bo = z*2 + k
    put_planes(v_ref.at[:, pl.ds(pl.multiple_of(bo*SEGR, 8), 512), :], unit(a_ref[...]))
    head = v_ref.at[:, pl.ds(pl.multiple_of(bo*SEGR, 8), 32), :]
    pz, pk = (pb % 8) // 2, (pb // 8) % 2
    remote(head, v_ref.at[:, pl.ds(pl.multiple_of((pz*2 + pk)*SEGR + 512, 8), 32), :], misc.at[1], (pb % 8, pb // 8), blk_no != 0)
    halo = v_ref.at[:, pl.ds(pl.multiple_of(bo*SEGR + 512, 8), 32), :]
    tv = pltpu.make_async_copy(tails.at[1], halo, misc.at[1])
    pl.when(blk_no == 127)(tv.start)

    def ring(q):
        for to in (dev(x, y, up, k), dev(x, y, dn, k), dev(x, y, z, 1 - k)):
            remote(vs(bo, q), vs(bo, q), got_v.at[bo, q], to)

    ring(0)
    ring(1)
    bu, bd, bf = up*2 + k, dn*2 + k, far*2 + k

    def near(q):
        for b, to, turn in ((bd, up, 0), (bu, dn, 1)):
            arrived(vs(b, q), got_v.at[b, q])
            if q % 2 == turn:
                remote(vs(b, q), vs(b, q), got_v.at[b, q], dev(x, y, to, k), guard=(0,))
            remote(vs(b, q), vs(b, q), got_v.at[b, q], dev(x, y, z, 1 - k), guard=(0,))

    def distant(q):
        arrived(vs(bf, q), got_v.at[bf, q])
        remote(vs(bf, q), vs(bf, q), got_v.at[bf, q], dev(x, y, z, 1 - k), guard=(0,))

    def others(q):
        for zz in range(4):
            b = zz*2 + 1 - k
            arrived(vs(b, q), got_v.at[b, q])

    def next_rows():
        pltpu.make_async_remote_copy(src_ref=u_ref.at[:, pl.ds(0, 32), :], dst_ref=u_ref.at[:, pl.ds(2048, 32), :], send_sem=misc.at[2], recv_sem=misc.at[0], device_id=dev(x, y, pr // 2, pr % 2), device_id_type=MESH).start()

    def stream(flag, cols, step):
        def blk(c, xc, d):
            return (cols[xc] // 2)*8 + ((y + d) % 4)*2 + c

        def get(c, xc, d):
            b = blk(c, xc, d)
            for h in range(2):
                arrived(us(b, h), got_u.at[b, h])
            if c == 0:
                pl.when(jnp.logical_and(b == 0, rb != 0))(next_rows)

        def put(c, xc, d, hs, *targets):
            b = blk(c, xc, d)
            for to in targets:
                for h in hs:
                    remote(us(b, h), us(b, h), got_u.at[b, h], to, guard=(0, flag))

        pl.when(flag)(lambda: step(get, put))

    def dx(p):
        return dev((x + p) % 4, y, z, k)

    def dy(p):
        return dev(x, (y + p) % 4, z, k)

    full = (0, 1)

    def h0(get, put):
        get(0, 0, 0)
        put(0, 0, 0, full, dx(1), dx(3))
        get(1, 0, 0)
        put(1, 0, 0, full, dy(1), dy(3))

    def h1(get, put):
        get(0, 0, 3)
        put(0, 0, 3, (0,), dy(1))
        put(0, 0, 3, full, dx(1), dx(3))
        get(0, 0, 1)
        put(0, 0, 1, (1,), dy(3))
        put(0, 0, 1, full, dx(1), dx(3))

    def h2(get, put):
        get(1, 1, 0)
        put(1, 1, 0, full, dy(1), dy(3))
        get(0, 0, 2)
        put(0, 0, 2, full, dx(1), dx(3))

    def yrelay(xc):
        def step(get, put):
            get(1, xc, 3)
            put(1, xc, 3, (0,), dy(1))
            get(1, xc, 1)
            put(1, xc, 1, (1,), dy(3))
        return step

    def h5(get, put):
        for xc in range(2):
            get(1, xc, 2)
        for d in range(4):
            get(0, 1, d)

    def away0(get, put):
        get(1, 0, 0)
        put(1, 0, 0, (0,), dx(1))
        put(1, 0, 0, full, dy(1), dy(3))
        get(1, 1, 0)
        put(1, 1, 0, (1,), dx(3))
        put(1, 1, 0, full, dy(1), dy(3))

    def away1(*ds):
        def step(get, put):
            for d in ds:
                get(0, 0, d)
                put(0, 0, d, (0,), dx(1))
                get(0, 1, d)
                put(0, 1, d, (1,), dx(3))
        return step

    def a5(get, put):
        for xc in range(2):
            get(1, xc, 2)

    hc = (x, (x + 2) % 4)
    ac = ((x + 3) % 4, (x + 1) % 4)

    def H(step):
        stream(home, hc, step)

    def A(step):
        stream(away, ac, step)

    H(h0)
    A(away0)
    near(0)
    ring(2)
    H(h1)
    A(away1(0))
    H(h2)
    A(yrelay(0))
    A(yrelay(1))
    near(1)
    tv.wait()
    ring(3)
    H(yrelay(0))
    A(away1(3))
    A(away1(1))
    H(yrelay(1))
    A(away1(2))
    H(h5)
    A(a5)
    tu = pltpu.make_async_copy(tails.at[0], u_ref.at[:, pl.ds(2048, 32), :], misc.at[0])
    pl.when(rb == 7)(tu.start)
    distant(0)
    distant(1)
    tu.wait()
    prep_rhs(u_ref, bt)
    others(0)
    near(2)
    others(1)

    def service(m):
        def first():
            near(3)
            distant(2)

        def third():
            distant(3)

        pl.when(m == 0)(first)
        pl.when(m == 1)(lambda: others(2))
        pl.when(m == 2)(third)
        pl.when(m == 3)(lambda: others(3))

    R = compute(v_ref, [a0, a1, a2], bt, [g0, g1, g2], acc, service)
    finish_rows(R, rowm)
    for c, when in waits:
        if when is None:
            c.wait_send()
        else:
            pl.when(when)(c.wait_send)
    pl.when(rb != 0)(lambda: arrived(u_ref.at[:, pl.ds(0, 32), :], misc.at[2]))
    for index, *how in later:
        if len(how) == 1:
            arrived(vs(0, 0), send.at[index])
        else:
            pl.when(how[1])(lambda index=index: arrived(us(0, 0), send.at[index]))
    cp = []
    for j in range(16):
        other = jnp.logical_or(col != j, away)
        c = pltpu.make_async_remote_copy(src_ref=rowm.at[j], dst_ref=rbuf.at[me_r], send_sem=rsend.at[j], recv_sem=rgot.at[me_r], device_id=(rb, j), device_id_type=MESH)
        pl.when(other)(c.start)
        cp.append((c, other))
    lr = pltpu.make_async_copy(rowm.at[col], rbuf.at[me_r], rgot.at[me_r])
    pl.when(home)(lr.start)
    finish_cols(acc, colm)
    for s in range(8):
        other = rb != s
        c = pltpu.make_async_remote_copy(src_ref=colm.at[s], dst_ref=cbuf.at[rb], send_sem=csend.at[s], recv_sem=cgot.at[rb], device_id=dev(x, y, s // 2, s % 2), device_id_type=MESH)
        pl.when(other)(c.start)
        cp.append((c, other))
    lc = pltpu.make_async_copy(colm.at[rb], cbuf.at[rb], cgot.at[rb])
    lc.start()
    for s in range(8):
        arrived(cbuf.at[s], cgot.at[s])
    for j in range(16):
        arrived(rbuf.at[j], rgot.at[j])
    colp_ref[...] = functools.reduce(jnp.maximum, [cbuf[s] for s in range(8)])
    rowp_ref[...] = functools.reduce(jnp.maximum, [rbuf[j] for j in range(16)])
    for c, other in cp:
        pl.when(other)(c.wait_send)

def on_device(stream, stream_tail, archive, archive_tail):
    DMA = pltpu.SemaphoreType.DMA
    col, row = pl.pallas_call(
        kern,
        out_shape=(jax.ShapeDtypeStruct((1, 512), F32), jax.ShapeDtypeStruct((1, 128), F32)),
        in_specs=[VM]*4, out_specs=(VM, VM),
        scratch_shapes=[
            pltpu.VMEM((2, 8*SEGR, 128), F32), pltpu.VMEM((2, 2176, 128), F32),
            pltpu.VMEM((2, 128, 128), F32), pltpu.VMEM((2, 2, 32, 128), F32),
            pltpu.VMEM((256, 512), jnp.bfloat16), pltpu.VMEM((256, 512), jnp.bfloat16), pltpu.VMEM((256, 512), jnp.bfloat16), pltpu.VMEM((C*BR, 512), jnp.bfloat16),
            pltpu.VMEM((256, C*128), F32), pltpu.VMEM((256, C*128), F32), pltpu.VMEM((256, C*128), F32),
            pltpu.VMEM((4096, 128), F32),
            pltpu.VMEM((8, 1, 512), F32), pltpu.VMEM((16, 1, 128), F32),
            pltpu.VMEM((8, 1, 512), F32), pltpu.VMEM((16, 1, 128), F32),
            DMA((140,)), DMA((8, NQ)), DMA((16, 2)), DMA((3,)),
            DMA((8,)), DMA((16,)), DMA((8,)), DMA((16,)),
        ],
        compiler_params=pltpu.CompilerParams(has_side_effects=True, collective_id=0, vmem_limit_bytes=67043328),
        name="join_profile")(stream, stream_tail, archive, archive_tail)
    return row.reshape(-1), col.reshape(-1)

def solution(mesh):
    return jax.shard_map(
        on_device, mesh=mesh,
        in_specs=(P(("row", "col"), None), P(), P(("col", "row"), None), P()),
        out_specs=(P(("row", "col")), P(("col", "row"))),
        check_vma=False)
```
